32 devices in a mesh: gx: 8 (over y, x, core), gy: 4 (over z).
Axes of the slice: x: 2, y: 2, z: 4, core: 2. Of those that a mesh axis runs over, the one named last changes fastest.
Arguments:
- fields: bfloat16 [128, 128, 256], P('gx', 'gy'), may hold values from -6 to 6
- w_down: bfloat16 [3, 3, 3, 32, 32], replicated, may hold values from -0.21875 to 0.21875
- w_pool: bfloat16 [2, 2, 2, 32, 64], replicated, may hold values from -0.375 to 0.375
- w_mid: bfloat16 [3, 3, 3, 64, 64], replicated, may hold values from -0.15625 to 0.15625
- w_unpool: bfloat16 [2, 2, 2, 64, 32], replicated, may hold values from -0.75 to 0.75
- w_up: bfloat16 [3, 3, 3, 32, 32], replicated, may hold values from -0.21875 to 0.21875
- cotangent: bfloat16 [128, 128, 256], P('gx', 'gy'), may hold values from -6 to 6
Outputs:
- output: bfloat16 [128, 128, 256], P('gx', 'gy')
- grad_fields: bfloat16 [128, 128, 256], P('gx', 'gy')
- grad_down: float32 [3, 3, 3, 32, 32], replicated
- grad_pool: float32 [2, 2, 2, 32, 64], replicated
- grad_mid: float32 [3, 3, 3, 64, 64], replicated
- grad_unpool: float32 [2, 2, 2, 64, 32], replicated
- grad_up: float32 [3, 3, 3, 32, 32], replicated
The draws below stay inside these ranges and needn't reach their ends.
All inputs are finite; a program needn't handle non-finite values.
Results may differ from the reference program's by a relative error of at most 0.0071.
Values may be sent and summed in bfloat16 or wider, within the bound.
A program may use at most 128 MiB of HBM per device.

```python
import math
import jax
import jax.numpy as jnp
from jax import lax

CF = 32
CC = 64
ZS = 8
NX = 128
NY = 128


def levels(stream_key, extent, split, low, high):
    def one(dim, shards_of):
        heights = jax.random.uniform(jax.random.fold_in(jax.random.fold_in(stream_key, 6), dim), (shards_of,), jnp.float32, low / len(split), high / len(split))
        return jnp.repeat(jnp.exp(heights), extent[dim] // shards_of).reshape((-1,) + (1,) * (len(extent) - dim - 1))

    level = one(*split[0])
    for cut in split[1:]:
        level = level * one(*cut)
    return level


def bell_draw(own_key, extent, scale, reach, cuts=(), held_as=jnp.bfloat16):
    result = jax.random.normal(own_key, extent, jnp.float32) * scale
    if len(cuts) > 0:
        result = levels(own_key, extent, cuts, -0.22, 0.18) * result
    return jnp.clip(result, min=-reach, max=reach).astype(held_as)


def setup_inputs(seed: int = 0) -> dict:
    key_of = jax.random.split(jax.random.key(seed), 8)
    return {
        "fields": bell_draw(key_of[0], (NX, NY, ZS * CF), 1.0, 6.0, ((0, 8), (1, 4))),
        "w_down": bell_draw(key_of[1], (3, 3, 3, CF, CF), (27 * CF) ** -0.5, 0.21875),
        "w_pool": bell_draw(key_of[2], (2, 2, 2, CF, CC), (8 * CF) ** -0.5, 0.375),
        "w_mid": bell_draw(key_of[3], (3, 3, 3, CC, CC), (27 * CC) ** -0.5, 0.15625),
        "w_unpool": bell_draw(key_of[4], (2, 2, 2, CC, CF), CC ** -0.5, 0.75),
        "w_up": bell_draw(key_of[5], (3, 3, 3, CF, CF), (27 * CF) ** -0.5, 0.21875),
        "cotangent": bell_draw(key_of[6], (NX, NY, ZS * CF), 1.0, 6.0, ((0, 8), (1, 4))),
    }


def dsilu(value):
    sig = jax.nn.sigmoid(value)
    return sig * (1.0 + value * (1.0 - sig))

def plane_shifts(planes):
    return jnp.stack([jnp.eye(planes, k=1 - kk, dtype=jnp.float32) for kk in range(3)])

def band_matrix(weight, planes):
    shifts = plane_shifts(planes)
    band = jnp.einsum('kpz,abkco->abpczo', shifts, weight.astype(jnp.float32))
    return band.reshape(3, 3, planes * weight.shape[3], planes * weight.shape[4]).astype(jnp.bfloat16)

def band_to_weight(dband, planes, cin, cout):
    shifts = plane_shifts(planes)
    return jnp.einsum('kpz,abpczo->abkco', shifts, dband.reshape(3, 3, planes, cin, planes, cout))

def flipped(weight):
    return jnp.transpose(weight[::-1, ::-1, ::-1], (0, 1, 2, 4, 3))

def wrap_pad(field):
    return jnp.pad(field, ((1, 1), (1, 1), (0, 0)), mode='wrap')

def conv_whole(field, weight, planes):
    band = band_matrix(weight, planes)
    padded = wrap_pad(field)
    xs, ys, width = field.shape
    total = jnp.zeros((xs * ys, band.shape[3]), jnp.float32)
    for aa in range(3):
        for bb in range(3):
            piece = padded[aa:aa + xs, bb:bb + ys, :].reshape(xs * ys, width)
            total = total + jnp.dot(piece, band[aa, bb], preferred_element_type=jnp.float32)
    return total.reshape(xs, ys, -1)

def conv_weight_grad(field, dout, planes, cin, cout):
    padded = wrap_pad(field)
    xs, ys, width = field.shape
    flat = dout.reshape(xs * ys, -1)
    parts = []
    for aa in range(3):
        for bb in range(3):
            piece = padded[aa:aa + xs, bb:bb + ys, :].reshape(xs * ys, width)
            parts.append(lax.dot_general(piece, flat, (((0,), (0,)), ((), ())), preferred_element_type=jnp.float32))
    return band_to_weight(jnp.stack(parts), planes, cin, cout)

def split_fine(field):
    xs, ys, width = field.shape
    parts = field.reshape(xs // 2, 2, ys // 2, 2, width).transpose(0, 2, 1, 3, 4)
    return parts.reshape(xs // 2 * (ys // 2), 4 * width)

def merge_fine(flat, xs, ys):
    width = flat.shape[1] // 4
    return flat.reshape(xs // 2, ys // 2, 2, 2, width).transpose(0, 2, 1, 3, 4).reshape(xs, ys, width)

def pool_matrix(weight, half):
    eye = jnp.eye(half, dtype=jnp.float32)
    mat = jnp.einsum('yz,ijlco->ijylczo', eye, weight.astype(jnp.float32))
    return mat.reshape(-1, half * weight.shape[4]).astype(jnp.bfloat16)

def unpool_matrix(weight, half):
    eye = jnp.eye(half, dtype=jnp.float32)
    mat = jnp.einsum('yz,ijlof->yoijzlf', eye, weight.astype(jnp.float32))
    return mat.reshape(half * weight.shape[3], -1).astype(jnp.bfloat16)

def reference(fields, w_down, w_pool, w_mid, w_unpool, w_up, cotangent):
    cf = w_down.shape[3]
    cc = w_mid.shape[3]
    xs, ys = (fields.shape[0], fields.shape[1])
    half = ZS // 2
    pmat = pool_matrix(w_pool, half)
    umat = unpool_matrix(w_unpool, half)
    pre_down = conv_whole(fields, w_down, ZS)
    hidden = jax.nn.silu(pre_down).astype(jnp.bfloat16)
    hidden_parts = split_fine(hidden)
    pre_pool = jnp.dot(hidden_parts, pmat, preferred_element_type=jnp.float32).reshape(xs // 2, ys // 2, -1)
    coarse = jax.nn.silu(pre_pool).astype(jnp.bfloat16)
    pre_mid = conv_whole(coarse, w_mid, half)
    middle = (coarse.astype(jnp.float32) + jax.nn.silu(pre_mid)).astype(jnp.bfloat16)
    middle_flat = middle.reshape(-1, middle.shape[2])
    lifted = jnp.dot(middle_flat, umat, preferred_element_type=jnp.float32)
    pre_up = hidden.astype(jnp.float32) + merge_fine(lifted, xs, ys)
    skip = jax.nn.silu(pre_up).astype(jnp.bfloat16)
    output = (fields.astype(jnp.float32) + conv_whole(skip, w_up, ZS)).astype(jnp.bfloat16)
    d_up = (conv_whole(cotangent, flipped(w_up), ZS) * dsilu(pre_up)).astype(jnp.bfloat16)
    d_up_parts = split_fine(d_up)
    d_middle = lax.dot_general(d_up_parts, umat, (((1,), (1,)), ((), ())), preferred_element_type=jnp.float32)
    d_middle = d_middle.reshape(xs // 2, ys // 2, -1)
    d_mid = (d_middle * dsilu(pre_mid)).astype(jnp.bfloat16)
    d_coarse = d_middle + conv_whole(d_mid, flipped(w_mid), half)
    d_pool = (d_coarse * dsilu(pre_pool)).astype(jnp.bfloat16)
    d_pool_flat = d_pool.reshape(-1, d_pool.shape[2])
    back = lax.dot_general(d_pool_flat, pmat, (((1,), (1,)), ((), ())), preferred_element_type=jnp.float32)
    d_hidden = d_up.astype(jnp.float32) + merge_fine(back, xs, ys)
    d_down = (d_hidden * dsilu(pre_down)).astype(jnp.bfloat16)
    grad_fields = (cotangent.astype(jnp.float32) + conv_whole(d_down, flipped(w_down), ZS)).astype(jnp.bfloat16)
    scale = 1.0 / math.sqrt(xs * ys * ZS)
    grad_up = conv_weight_grad(skip, cotangent, ZS, cf, cf) * scale
    grad_mid = conv_weight_grad(coarse, d_mid, half, cc, cc) * scale
    grad_down = conv_weight_grad(fields, d_down, ZS, cf, cf) * scale
    eye = jnp.eye(half, dtype=jnp.float32)
    d_umat = lax.dot_general(middle_flat, d_up_parts, (((0,), (0,)), ((), ())), preferred_element_type=jnp.float32)
    grad_unpool = jnp.einsum('yz,yoijzlf->ijlof', eye, d_umat.reshape(half, cc, 2, 2, half, 2, cf)) * scale
    d_pmat = lax.dot_general(hidden_parts, d_pool_flat, (((0,), (0,)), ((), ())), preferred_element_type=jnp.float32)
    grad_pool = jnp.einsum('yz,ijylczo->ijlco', eye, d_pmat.reshape(2, 2, half, 2, cf, half, cc)) * scale
    return (output, grad_fields, grad_down, grad_pool, grad_mid, grad_unpool, grad_up)
```

```python
import functools
import math

import jax
import jax.numpy as jnp
from jax import lax
from jax.experimental import pallas as pl
from jax.experimental.pallas import tpu as pltpu
from jax.sharding import PartitionSpec as P

BF16 = jnp.bfloat16
F32 = jnp.float32
MESH = pl.DeviceIdType.MESH
LANES = 128
ROWS = 16


def dot(left, right):
    return lax.dot_general(left, right, (((1,), (0,)), ((), ())), preferred_element_type=F32)


def dot_t(left, right):
    return lax.dot_general(left, right, (((1,), (1,)), ((), ())), preferred_element_type=F32)


def iota(shape, dim):
    return lax.broadcasted_iota(jnp.int32, shape, dim)


def div(value, by):
    return lax.div(value, jnp.int32(by))


def rem(value, by):
    return lax.rem(value, jnp.int32(by))


def one_hot(mask):
    return jnp.where(mask, 1.0, 0.0).astype(BF16)


def silu_parts(value):
    sig = jax.nn.sigmoid(value)
    return value * sig, sig * (1.0 + value * (1.0 - sig))


def split_matrix(xh, ys, parity):
    hy = ys // 2
    shape = (xh * hy, xh * ys)
    row, col = iota(shape, 0), iota(shape, 1)
    return one_hot(col == div(row, hy) * ys + rem(row, hy) * 2 + parity)


def merge_matrix(xh, ys, parity):
    hy = ys // 2
    shape = (xh * ys, xh * hy)
    row, col = iota(shape, 0), iota(shape, 1)
    same = col == div(row, ys) * hy + div(rem(row, ys), 2)
    return one_hot(same & (rem(row, 2) == parity))


def shift_matrix(rows, hy, step):
    row, col = iota((rows, rows), 0), iota((rows, rows), 1)
    edge = hy - 1 if step > 0 else 0
    return one_hot((col == row + step) & (rem(row, hy) != edge))


def place_matrix(count, part, hy, step):
    rows = (count + 2) // 2 * hy
    shape = (rows, 3 * ROWS)
    row, col = iota(shape, 0), iota(shape, 1)
    across = div(row, hy) + part * ((count + 2) // 2)
    edge = hy - 1 if step > 0 else 0
    wanted = jnp.where(
        across == 0, count - 1, jnp.where(across == count + 1, 2 * ROWS, across + ROWS - 1)
    )
    return one_hot((rem(row, hy) == edge) & (col == wanted))


def edge_matrix(count, hy, last):
    shape = (ROWS, count * hy)
    row, col = iota(shape, 0), iota(shape, 1)
    return one_hot(col == row * hy + (hy - 1 if last else 0))


def tile_matrix(small, width):
    shape = (small, width)
    return one_hot(rem(iota(shape, 1), small) == iota(shape, 0))


def build_band(weight, band, planes, chan, width):
    tile = tile_matrix(chan, width)
    plane = div(iota((chan, width), 1), chan)

    def step(tap, carry):
        start = pl.multiple_of(tap * (3 * chan), ROWS)
        wide = dot(weight[pl.ds(start, 3 * chan), :], tile)
        parts = [wide[kk * chan : (kk + 1) * chan] for kk in range(3)]
        for pp in range(planes):
            block = jnp.zeros((chan, width), F32)
            for kk in range(3):
                block = jnp.where(plane == pp + 1 - kk, parts[kk], block)
            band[tap, pp * chan : (pp + 1) * chan, :] = block.astype(BF16)
        return carry

    lax.fori_loop(0, 9, step, 0)


def build_pool(weight, mats, half, cf, cc, width):
    wide = dot(weight[...], tile_matrix(cc, width))
    plane = div(iota((2 * cf, width), 1), cc)
    for ij in range(4):
        part = wide[ij * 2 * cf : (ij + 1) * 2 * cf]
        for zz in range(half):
            block = jnp.where(plane == zz, part, 0.0)
            mats[ij, zz * 2 * cf : (zz + 1) * 2 * cf, :] = block.astype(BF16)


def build_unpool(weight, mats, half, cf, cc, width):
    wide = dot(weight[...], tile_matrix(cf, width))
    lane = iota((cc, width), 1)
    plane = div(lane, 2 * cf)
    upper = rem(div(lane, cf), 2) == 1
    for ij in range(4):
        low = wide[2 * ij * cc : (2 * ij + 1) * cc]
        high = wide[(2 * ij + 1) * cc : (2 * ij + 2) * cc]
        part = jnp.where(upper, high, low)
        for zz in range(half):
            block = jnp.where(plane == zz, part, 0.0)
            mats[ij, zz * cc : (zz + 1) * cc, :] = block.astype(BF16)


def parity_rows(value, hx, hy, side):
    width = value.shape[-1]
    return value.reshape(hx, 2, hy, width)[:, side].reshape(hx * hy, width)


def woven_rows(first, second, hx, hy):
    width = first.shape[-1]
    both = jnp.concatenate(
        [first.reshape(hx, 1, hy, width), second.reshape(hx, 1, hy, width)], axis=1
    )
    return both.reshape(2 * hx * hy, width)


def folded(block, chan):
    total = block[:, :LANES]
    for part in range(1, block.shape[1] // LANES):
        total = total + block[:, part * LANES : (part + 1) * LANES]
    step = LANES // 2
    while step >= chan:
        total = total + pltpu.roll(total, step, 1)
        step //= 2
    return total


class Packer:
    def __init__(self, target, row, chan):
        self.target, self.row, self.chan = target, row, chan
        self.per = LANES // chan
        self.group = div(iota((chan, LANES), 1), chan)
        self.held, self.count = None, 0

    def add(self, value):
        spot = self.count % self.per
        self.held = value if spot == 0 else jnp.where(self.group == spot, value, self.held)
        self.count += 1
        if spot == self.per - 1:
            self.flush()

    def flush(self):
        if self.held is not None:
            self.target[self.row : self.row + self.chan, :] = self.held.astype(BF16)
            self.row += self.chan
            self.held = None
        return self.row


def conv_grad(parts, tap_of, planes, chan, width, packer):
    plane = div(iota((chan, width), 1), chan)
    for tap in range(9):
        dband = None
        for index, part in enumerate(parts):
            term = dot(part, tap_of(index, tap // 3, tap % 3))
            dband = term if dband is None else dband + term
        for kk in range(3):
            total = jnp.zeros((chan, width), F32)
            for zz in range(planes):
                if 0 <= zz + kk - 1 < planes:
                    rows = dband[zz * chan : (zz + 1) * chan]
                    total = jnp.where(plane == zz + kk - 1, rows, total)
            packer.add(folded(total, chan))
    return packer.flush()


def pair_grad(left_t, rights, half, chan, width, packer):
    plane = div(iota((chan, width), 1), width // half)
    for right in rights:
        full = dot(left_t, right)
        total = jnp.zeros((chan, width), F32)
        for zz in range(half):
            total = jnp.where(plane == zz, full[zz * chan : (zz + 1) * chan], total)
        packer.add(folded(total, width // half))
    return packer.flush()


def turned(value):
    return value.astype(F32).T.astype(BF16)


def main_kernel(
    dims, fields, w_down, w_pool, w_mid, w_unpool, w_up, cot,
    out_s, gf_s, grads,
    fc, sk, dd, co, dm,
    fc_send, sk_send, dd_send, co_send, dm_send,
    fc_recv, sk_recv, dd_recv, co_recv, dm_recv,
    b_down, b_up, b_mid, p_mat, u_mat,
    shift, place, place_c,
    hid, ds_down, g_up, d_up, cot_t,
    sum0, sum1, sum2, got0, got1, got2, mid0, mid1, mid2,
    ex_send, ex_recv, s1, r1, s2, r2, s3, r3,
):
    nx, ny, xs, ys, cf, cc, planes, scale, sizes = dims
    half, hx, hy = planes // 2, xs // 2, ys // 2
    width = planes * cf
    cells, ccells = xs * hy, hx * hy
    ix, iy = lax.axis_index("gx"), lax.axis_index("gy")

    def at(dx, dy):
        return {"gx": lax.rem(ix + (dx + nx), nx), "gy": lax.rem(iy + (dy + ny), ny)}

    partners = [(dx, 0) for dx in range(1, nx)] + [(0, dy) for dy in range(1, ny)]
    partners += [(dx, dy) for dx in (-1, 1) for dy in (-1, 1)]
    barrier = pltpu.get_barrier_semaphore()
    for dx, dy in partners:
        pl.semaphore_signal(barrier, inc=1, device_id=at(dx, dy), device_id_type=MESH)

    def send(src, dst, ssem, rsem, dx, dy):
        copy = pltpu.make_async_remote_copy(
            src_ref=src, dst_ref=dst, send_sem=ssem, recv_sem=rsem,
            device_id=at(dx, dy), device_id_type=MESH,
        )
        copy.start()
        return copy

    def exchange(number, buf, snd, rcv, count, low, high):
        ss, rs = ex_send.at[number], ex_recv.at[number]
        copies = []
        for dx in (-1, 0, 1):
            rows = pl.ds((1 - dx) * ROWS, ROWS)
            for side, dy in ((0, -1), (1, 1)):
                spot = 2 * (dx + 1) + side
                copies.append(
                    send(snd.at[side], rcv.at[side, :, rows, :], ss.at[spot], rs.at[spot], dx, dy)
                )
        for spot, dx, src, dst in ((6, -1, 1, count + 1), (7, 1, count, 0)):
            copies.append(
                send(
                    buf.at[:, src, :, low:high], buf.at[:, dst, :, low:high],
                    ss.at[spot], rs.at[spot], dx, 0,
                )
            )
        return copies

    def arrive(copies):
        for copy in copies:
            copy.wait_recv()

    def shifts(buf, rcv, index, count, up_from, up_to, down_from, down_to, places):
        part = (count + 2) // 2
        rows = part * hy
        for hh in range(2):
            span = slice(hh * part, (hh + 1) * part)
            for side, start, stop in ((0, up_from, up_to), (1, down_from, down_to)):
                own = buf[index, span, :, start : start + width].reshape(rows, width)
                moved = dot(shift[side, :rows, :rows], own)
                moved = moved + dot(places[side, hh], rcv[side, index])
                buf[index, span, :, stop : stop + width] = moved.astype(BF16).reshape(
                    part, hy, width
                )

    def fine_shifts(buf, rcv, index=0):
        shifts(buf, rcv, index, xs, width, 3 * width, 2 * width, 0, place)

    def coarse_shifts(buf, rcv):
        shifts(buf, rcv, 0, hx, width, 2 * width, width, 0, place_c)

    def tap(buf, index, count, aa, lane):
        return buf[index, aa : aa + count, :, lane : lane + width].reshape(count * hy, width)

    def conv(buf, index, count, jj, band):
        total = None
        for aa in range(3):
            left = buf[index, aa : aa + count, :, jj * width : (jj + 3) * width]
            term = dot(
                left.reshape(count * hy, 3 * width),
                band[3 * aa : 3 * aa + 3].reshape(3 * width, width),
            )
            total = term if total is None else total + term
        return total

    def conv_t(buf, index, count, jj, band):
        total = None
        for aa in range(3):
            for bb in range(3):
                left = tap(buf, index, count, aa, (jj + bb) * width)
                term = dot_t(left, band[3 * (2 - aa) + 2 - bb])
                total = term if total is None else total + term
        return total

    def edges(buf, snd, index, count, low, high):
        for side, lane in ((0, low), (1, high)):
            own = tap(buf, index, count, 1, lane)
            snd[side, index] = dot(edge_matrix(count, hy, side == 1), own).astype(BF16)

    for parity in range(2):
        pick = split_matrix(hx, ys, parity)
        for index, ref in ((0, fields), (1, cot)):
            for hh in range(2):
                rows = ref[hh * hx * ys : (hh + 1) * hx * ys, :]
                lane = (1 + parity) * width
                fc[index, 1 + hh * hx : 1 + (hh + 1) * hx, :, lane : lane + width] = (
                    dot(pick, rows).astype(BF16).reshape(hx, hy, width)
                )
    for index in range(2):
        edges(fc, fc_send, index, xs, width, 2 * width)
    pl.semaphore_wait(barrier, len(partners))
    moving = exchange(0, fc, fc_send, fc_recv, xs, width, 3 * width)

    part = (xs + 2) // 2 * hy
    for side, step in ((0, 1), (1, -1)):
        shift[side] = shift_matrix(part, hy, step)
        for hh in range(2):
            place[side, hh] = place_matrix(xs, hh, hy, step)
            place_c[side, hh] = place_matrix(hx, hh, hy, step)
    build_band(w_down, b_down, planes, cf, width)
    build_pool(w_pool, p_mat, half, cf, cc, width)
    build_band(w_up, b_up, planes, cf, width)
    for jj in range(2):
        cot_t[jj] = turned(tap(fc, 1, xs, 1, (1 + jj) * width))

    arrive(moving)
    sends = list(moving)
    fine_shifts(fc, fc_recv, 0)
    for jj in range(2):
        value, slope = silu_parts(conv(fc, 0, xs, jj, b_down))
        hid[jj] = value.astype(BF16)
        ds_down[jj] = slope
    pre_pool = None
    for jj in range(2):
        for ii in range(2):
            term = dot(parity_rows(hid[jj], hx, hy, ii), p_mat[2 * ii + jj])
            pre_pool = term if pre_pool is None else pre_pool + term
    coarse, ds_pool = silu_parts(pre_pool)
    co[0, 1 : hx + 1, :, width : 2 * width] = coarse.astype(BF16).reshape(hx, hy, width)
    edges(co, co_send, 0, hx, width, width)
    moving = exchange(1, co, co_send, co_recv, hx, width, 2 * width)

    build_band(w_mid, b_mid, half, cc, width)
    build_unpool(w_unpool, u_mat, half, cf, cc, width)
    fine_shifts(fc, fc_recv, 1)
    for jj in range(2):
        g_up[jj] = conv_t(fc, 1, xs, jj, b_up)

    arrive(moving)
    sends += moving
    coarse_shifts(co, co_recv)
    value, ds_mid = silu_parts(conv(co, 0, hx, 0, b_mid))
    own = tap(co, 0, hx, 1, width).astype(F32)
    middle = (own + value).astype(BF16)
    d_middle = None
    for jj in range(2):
        lifted = [dot(middle, u_mat[2 * ii + jj]) for ii in range(2)]
        pre_up = hid[jj].astype(F32) + woven_rows(lifted[0], lifted[1], hx, hy)
        value, slope = silu_parts(pre_up)
        lane = (1 + jj) * width
        sk[0, 1 : xs + 1, :, lane : lane + width] = value.astype(BF16).reshape(xs, hy, width)
        d_up[jj] = (g_up[jj] * slope).astype(BF16)
        for ii in range(2):
            term = dot_t(parity_rows(d_up[jj], hx, hy, ii), u_mat[2 * ii + jj])
            d_middle = term if d_middle is None else d_middle + term
    d_mid = (d_middle * ds_mid).astype(BF16)
    dm[0, 1 : hx + 1, :, width : 2 * width] = d_mid.reshape(hx, hy, width)
    edges(dm, dm_send, 0, hx, width, width)
    moving = exchange(2, dm, dm_send, dm_recv, hx, width, 2 * width)
    edges(sk, sk_send, 0, xs, width, 2 * width)
    skips = exchange(3, sk, sk_send, sk_recv, xs, width, 3 * width)

    class Reduction:
        def __init__(self, group, terms, got, mids, base):
            self.group, self.terms, self.got, self.mids, self.base = group, terms, got, mids, base
            self.rows = sizes[group] // nx

        def piece(self, index):
            return pl.ds(pl.multiple_of(index * self.rows, ROWS), self.rows)

        def scatter(self):
            self.copies = []
            for dx in range(1, nx):
                target = at(dx, 0)["gx"]
                self.copies.append(
                    send(
                        self.terms.at[self.piece(target), :], self.got.at[dx - 1],
                        s1.at[self.group, dx - 1], r1.at[self.group, dx - 1], dx, 0,
                    )
                )
            return self.copies

        def across(self):
            arrive(self.copies)
            total = self.terms[self.piece(ix), :].astype(F32)
            for dx in range(1, nx):
                total = total + self.got[dx - 1].astype(F32)
            self.mids[iy] = total.astype(BF16)
            self.copies = []
            for dy in range(1, ny):
                self.copies.append(
                    send(
                        self.mids.at[iy], self.mids.at[iy],
                        s2.at[self.group, dy - 1], r2.at[self.group, dy - 1], 0, dy,
                    )
                )
            return self.copies

        def gather(self):
            arrive(self.copies)
            total = self.mids[0].astype(F32)
            for yy in range(1, ny):
                total = total + self.mids[yy].astype(F32)
            start = pl.multiple_of(self.base + ix * self.rows, ROWS)
            mine = pl.ds(start, self.rows)
            grads[mine, :] = (total * scale).astype(BF16)
            self.copies = []
            for dx in range(1, nx):
                self.copies.append(
                    send(
                        grads.at[mine, :], grads.at[mine, :],
                        s3.at[self.group, dx - 1], r3.at[self.group, dx - 1], dx, 0,
                    )
                )
            return self.copies

    def padded_tail(ref, row, group):
        if row < sizes[group]:
            ref[row:, :] = jnp.zeros((sizes[group] - row, LANES), BF16)

    row = conv_grad(
        [turned(d_mid)], lambda index, aa, bb: tap(co, 0, hx, aa, bb * width),
        half, cc, width, Packer(sum0, 0, cc),
    )
    padded_tail(sum0, row, 0)
    red0 = Reduction(0, sum0, got0, mid0, 0)
    sends += red0.scatter()

    arrive(moving)
    sends += moving
    coarse_shifts(dm, dm_recv)
    d_coarse = d_middle + conv_t(dm, 0, hx, 0, b_mid)
    d_pool = (d_coarse * ds_pool).astype(BF16)
    for jj in range(2):
        back = [dot_t(d_pool, p_mat[2 * ii + jj]) for ii in range(2)]
        d_hidden = d_up[jj].astype(F32) + woven_rows(back[0], back[1], hx, hy)
        lane = (1 + jj) * width
        d_down = (d_hidden * ds_down[jj]).astype(BF16)
        dd[0, 1 : xs + 1, :, lane : lane + width] = d_down.reshape(xs, hy, width)
    edges(dd, dd_send, 0, xs, width, 2 * width)
    moving = exchange(4, dd, dd_send, dd_recv, xs, width, 3 * width)

    downs = [turned(tap(dd, 0, xs, 1, (1 + jj) * width)) for jj in range(2)]
    row = conv_grad(
        downs, lambda jj, aa, bb: tap(fc, 0, xs, aa, (jj + bb) * width),
        planes, cf, width, Packer(sum2, 0, cf),
    )
    row = pair_grad(
        turned(d_pool),
        [parity_rows(hid[jj], hx, hy, ii) for ii in range(2) for jj in range(2)],
        half, cc, width, Packer(sum2, row, cc),
    )
    padded_tail(sum2, row, 2)
    red2 = Reduction(2, sum2, got2, mid2, sizes[0] + sizes[1])
    sends += red2.scatter()
    sends += red0.across()

    arrive(skips)
    sends += skips
    fine_shifts(sk, sk_recv)
    row = conv_grad(
        [cot_t[0], cot_t[1]], lambda jj, aa, bb: tap(sk, 0, xs, aa, (jj + bb) * width),
        planes, cf, width, Packer(sum1, 0, cf),
    )
    row = pair_grad(
        turned(middle),
        [parity_rows(d_up[jj], hx, hy, ii) for ii in range(2) for jj in range(2)],
        half, cc, width, Packer(sum1, row, cc),
    )
    padded_tail(sum1, row, 1)
    red1 = Reduction(1, sum1, got1, mid1, sizes[0])
    sends += red1.scatter()
    sends += red2.across()
    sends += red0.gather()

    for jj in range(2):
        own = tap(fc, 0, xs, 1, (1 + jj) * width).astype(F32)
        out_s[jj] = (own + conv(sk, 0, xs, jj, b_up)).astype(BF16)
    sends += red1.across()
    sends += red2.gather()
    arrive(moving)
    sends += moving
    fine_shifts(dd, dd_recv)
    for jj in range(2):
        own = tap(fc, 1, xs, 1, (1 + jj) * width).astype(F32)
        gf_s[jj] = (own + conv_t(dd, 0, xs, jj, b_down)).astype(BF16)
    sends += red1.gather()
    for red in (red0, red1, red2):
        arrive(red.copies)
    for copy in sends:
        copy.wait_send()


def last_kernel(
    dims, out_s, gf_s, grads, output, grad_fields, g_down, g_pool, g_mid, g_unpool, g_up
):
    nx, ny, xs, ys, cf, cc, planes, scale, sizes = dims
    hx, hy = xs // 2, ys // 2
    merge = [merge_matrix(hx, ys, parity) for parity in range(2)]
    for source, target in ((out_s, output), (gf_s, grad_fields)):
        for hh in range(2):
            rows = slice(hh * hx * hy, (hh + 1) * hx * hy)
            value = dot(merge[0], source[0, rows, :]) + dot(merge[1], source[1, rows, :])
            target[hh * hx * ys : (hh + 1) * hx * ys, :] = value.astype(BF16)

    def unpack(row, chan, target):
        done, total = 0, target.shape[0]
        while done < total:
            block = grads[row : row + chan, :].astype(F32).T
            count = min(LANES, total - done)
            target[done : done + count, :] = block[:count]
            row, done = row + chan, done + count
        return row

    unpack(0, cc, g_mid)
    row = unpack(sizes[0], cf, g_up)
    for pair in range(2):
        block = grads[row : row + cc, :].astype(F32)
        for part in range(4):
            moved = block if part == 0 else pltpu.roll(block, LANES - part * cf, 1)
            first = (pair * 4 + part) * cc
            g_unpool[first : first + cc, :] = moved[:, :cf]
        row += cc
    row = unpack(sizes[0] + sizes[1], cf, g_down)
    unpack(row, cc, g_pool)


def per_device(dims, fields, w_down, w_pool, w_mid, w_unpool, w_up, cotangent):
    nx, ny, xs, ys, cf, cc, planes, scale, sizes = dims
    hx, hy = xs // 2, ys // 2
    width = planes * cf
    cells = xs * hy
    vmem = pl.BlockSpec(memory_space=pltpu.VMEM)

    def fine(lead=1):
        return pltpu.VMEM((lead, xs + 2, hy, 4 * width), BF16)

    def coarse():
        return pltpu.VMEM((1, hx + 2, hy, 3 * width), BF16)

    def sent(lead=1):
        return pltpu.VMEM((2, lead, ROWS, width), BF16)

    def taken(lead=1):
        return pltpu.VMEM((2, lead, 3 * ROWS, width), BF16)

    def sems(*shape):
        return pltpu.SemaphoreType.DMA(shape)

    part, part_c = (xs + 2) // 2 * hy, (hx + 2) // 2 * hy
    rows = [size // nx for size in sizes]
    split = jax.ShapeDtypeStruct((2, cells, width), BF16)
    out_s, gf_s, grads = pl.pallas_call(
        functools.partial(main_kernel, dims),
        out_shape=(split, split, jax.ShapeDtypeStruct((sum(sizes), LANES), BF16)),
        in_specs=[vmem] * 7,
        out_specs=(vmem,) * 3,
        scratch_shapes=[
            fine(2), fine(), fine(), coarse(), coarse(),
            sent(2), sent(), sent(), sent(), sent(),
            taken(2), taken(), taken(), taken(), taken(),
            pltpu.VMEM((9, width, width), BF16),
            pltpu.VMEM((9, width, width), BF16),
            pltpu.VMEM((9, width, width), BF16),
            pltpu.VMEM((4, width, width), BF16),
            pltpu.VMEM((4, width, width), BF16),
            pltpu.VMEM((2, part, part), BF16),
            pltpu.VMEM((2, 2, part, 3 * ROWS), BF16),
            pltpu.VMEM((2, 2, part_c, 3 * ROWS), BF16),
            pltpu.VMEM((2, cells, width), BF16),
            pltpu.VMEM((2, cells, width), F32),
            pltpu.VMEM((2, cells, width), F32),
            pltpu.VMEM((2, cells, width), BF16),
            pltpu.VMEM((2, width, cells), BF16),
            *[pltpu.VMEM((size, LANES), BF16) for size in sizes],
            *[pltpu.VMEM((nx - 1, row, LANES), BF16) for row in rows],
            *[pltpu.VMEM((ny, row, LANES), BF16) for row in rows],
            sems(5, 8), sems(5, 8),
            sems(3, nx - 1), sems(3, nx - 1),
            sems(3, ny - 1), sems(3, ny - 1),
            sems(3, nx - 1), sems(3, nx - 1),
        ],
        compiler_params=pltpu.CompilerParams(
            collective_id=0, has_side_effects=True, vmem_limit_bytes=56 << 20
        ),
        name="unet",
    )(
        fields.reshape(xs * ys, width),
        w_down.reshape(-1, cf),
        w_pool.reshape(-1, cc),
        w_mid.reshape(-1, cc),
        w_unpool.reshape(-1, cf),
        w_up.reshape(-1, cf),
        cotangent.reshape(xs * ys, width),
    )

    def f32(*shape):
        return jax.ShapeDtypeStruct(shape, F32)

    flat = jax.ShapeDtypeStruct((xs * ys, width), BF16)
    results = pl.pallas_call(
        functools.partial(last_kernel, dims),
        out_shape=(
            flat, flat, f32(27 * cf, cf), f32(8 * cf, cc), f32(27 * cc, cc),
            f32(8 * cc, cf), f32(27 * cf, cf),
        ),
        in_specs=[vmem] * 3,
        out_specs=(vmem,) * 7,
        name="layouts",
    )(out_s, gf_s, grads)
    shapes = [
        fields.shape, fields.shape, w_down.shape, w_pool.shape, w_mid.shape, w_unpool.shape,
        w_up.shape,
    ]
    return tuple(value.reshape(shape) for value, shape in zip(results, shapes))


def solution(mesh):
    nx, ny = mesh.shape["gx"], mesh.shape["gy"]

    def whole(fields, w_down, w_pool, w_mid, w_unpool, w_up, cotangent):
        cf, cc = w_down.shape[3], w_mid.shape[3]
        xs, ys = fields.shape[0] // nx, fields.shape[1] // ny
        planes = fields.shape[2] // cf
        scale = 1.0 / math.sqrt(fields.shape[0] * fields.shape[1] * planes)

        def blocks(taps, chan):
            return -(-taps * chan // LANES) * chan

        fine_rows = blocks(27, cf)
        pair_rows = 4 * cc * 2 * cf // LANES
        unit = ROWS * nx
        sizes = tuple(
            -(-rows // unit) * unit
            for rows in (blocks(27, cc), fine_rows + pair_rows, fine_rows + pair_rows)
        )
        dims = (nx, ny, xs, ys, cf, cc, planes, scale, sizes)
        placed = (P("gx", "gy", None), P(), P(), P(), P(), P(), P("gx", "gy", None))
        return jax.shard_map(
            functools.partial(per_device, dims),
            mesh=mesh,
            in_specs=placed,
            out_specs=(P("gx", "gy", None), P("gx", "gy", None), P(), P(), P(), P(), P()),
            check_vma=False,
        )(fields, w_down, w_pool, w_mid, w_unpool, w_up, cotangent)

    return whole
```

```python
import functools
import math

import jax
import jax.numpy as jnp
from jax import lax
from jax.experimental import pallas as pl
from jax.experimental.pallas import tpu as pltpu
from jax.sharding import PartitionSpec as P

BF16 = jnp.bfloat16
F32 = jnp.float32
MESH = pl.DeviceIdType.MESH
LANES = 128
ROWS = 16


def dot(left, right):
    return lax.dot_general(left, right, (((1,), (0,)), ((), ())), preferred_element_type=F32)


def dot_t(left, right):
    return lax.dot_general(left, right, (((1,), (1,)), ((), ())), preferred_element_type=F32)


def iota(shape, dim):
    return lax.broadcasted_iota(jnp.int32, shape, dim)


def div(value, by):
    return lax.div(value, jnp.int32(by))


def rem(value, by):
    return lax.rem(value, jnp.int32(by))


def one_hot(mask):
    return jnp.where(mask, 1.0, 0.0).astype(BF16)


def silu_parts(value):
    sig = jax.nn.sigmoid(value)
    return value * sig, sig * (1.0 + value * (1.0 - sig))


def row_matrix(xs, ys):
    hx = xs // 2
    shape = (xs * ys, xs * ys)
    row, col = iota(shape, 0), iota(shape, 1)
    place = rem(row, xs)
    across = rem(place, hx) * 2 + div(place, hx)
    return one_hot(col == across * ys + div(row, xs))


def row_matrix_back(xs, ys):
    hx = xs // 2
    shape = (xs * ys, xs * ys)
    row, col = iota(shape, 0), iota(shape, 1)
    across = div(row, ys)
    return one_hot(col == rem(row, ys) * xs + rem(across, 2) * hx + div(across, 2))


def fine_shift(lines, xs, step):
    hx = xs // 2
    shape = (lines * xs, lines * xs)
    row, col = iota(shape, 0), iota(shape, 1)
    place = rem(row, xs)
    first = place < hx
    if step > 0:
        wanted = jnp.where(first, row + hx, row - hx + 1)
        edge = xs - 1
    else:
        wanted = jnp.where(first, row + hx - 1, row - hx)
        edge = 0
    return one_hot((col == wanted) & (place != edge))


def coarse_shift(lines, hx, step):
    shape = (lines * hx, lines * hx)
    row, col = iota(shape, 0), iota(shape, 1)
    edge = hx - 1 if step > 0 else 0
    return one_hot((col == row + step) & (rem(row, hx) != edge))


def halo_matrix(lines, across, depth, base, step):
    shape = (lines * across, depth)
    row, col = iota(shape, 0), iota(shape, 1)
    edge = across - 1 if step > 0 else 0
    return one_hot((rem(row, across) == edge) & (col == div(row, across) + base))


def edge_matrix(rows, lines, across, base):
    shape = (2 * rows, lines * across)
    row, col = iota(shape, 0), iota(shape, 1)
    first = row < rows
    line = jnp.where(first, row, row - rows) - base
    return one_hot(col == line * across + jnp.where(first, 0, across - 1))


def tile_matrix(small, width):
    shape = (small, width)
    return one_hot(rem(iota(shape, 1), small) == iota(shape, 0))


def build_band(weight, band, planes, chan, width):
    tile = tile_matrix(chan, width)
    plane = div(iota((chan, width), 1), chan)

    def step(tap, carry):
        start = pl.multiple_of(tap * (3 * chan), ROWS)
        wide = dot(weight[pl.ds(start, 3 * chan), :], tile)
        spot = rem(tap, 3) * 3 + div(tap, 3)
        parts = [wide[kk * chan : (kk + 1) * chan] for kk in range(3)]
        for pp in range(planes):
            block = jnp.zeros((chan, width), F32)
            for kk in range(3):
                block = jnp.where(plane == pp + 1 - kk, parts[kk], block)
            band[spot, pp * chan : (pp + 1) * chan, :] = block.astype(BF16)
        return carry

    lax.fori_loop(0, 9, step, 0)


def build_pool(weight, mats, half, cf, cc, width):
    wide = dot(weight[...], tile_matrix(cc, width))
    plane = div(iota((2 * cf, width), 1), cc)
    for ij in range(4):
        part = wide[ij * 2 * cf : (ij + 1) * 2 * cf]
        for zz in range(half):
            block = jnp.where(plane == zz, part, 0.0)
            mats[ij, zz * 2 * cf : (zz + 1) * 2 * cf, :] = block.astype(BF16)


def folded(block, chan):
    total = block[:, :LANES]
    for part in range(1, block.shape[1] // LANES):
        total = total + block[:, part * LANES : (part + 1) * LANES]
    step = LANES // 2
    while step >= chan:
        total = total + pltpu.roll(total, step, 1)
        step //= 2
    return total


class Packer:
    def __init__(self, target, row, chan):
        self.target, self.row, self.chan = target, row, chan
        self.per = LANES // chan
        self.group = div(iota((chan, LANES), 1), chan)
        self.held, self.count = None, 0

    def add(self, value):
        spot = self.count % self.per
        self.held = value if spot == 0 else jnp.where(self.group == spot, value, self.held)
        self.count += 1
        if spot == self.per - 1:
            self.flush()

    def flush(self):
        if self.held is not None:
            self.target[self.row : self.row + self.chan, :] = self.held.astype(BF16)
            self.row += self.chan
            self.held = None
        return self.row


def conv_grad(parts, tap_of, planes, chan, width, packer, sign=1):
    plane = div(iota((chan, width), 1), chan)
    for tap in range(9):
        dband = None
        for index, part in enumerate(parts):
            term = dot(part, tap_of(index, tap // 3, tap % 3))
            dband = term if dband is None else dband + term
        for kk in range(3):
            total = jnp.zeros((chan, width), F32)
            for zz in range(planes):
                lane = zz + sign * (kk - 1)
                if 0 <= lane < planes:
                    rows = dband[zz * chan : (zz + 1) * chan]
                    total = jnp.where(plane == lane, rows, total)
            packer.add(folded(total, chan))
    return packer.flush()


def pair_grad(left_t, rights, half, chan, width, packer):
    plane = div(iota((chan, width), 1), width // half)
    for right in rights:
        full = dot(left_t, right)
        total = jnp.zeros((chan, width), F32)
        for zz in range(half):
            total = jnp.where(plane == zz, full[zz * chan : (zz + 1) * chan], total)
        packer.add(folded(total, width // half))
    return packer.flush()


def turned(value):
    return value.astype(F32).T.astype(BF16)


def turned_blocks(source, row, chan, target):
    done, total = 0, target.shape[0]
    while done < total:
        block = source[row : row + chan, :].astype(F32).T
        count = min(LANES, total - done)
        target[done : done + count, :] = block[:count]
        row, done = row + chan, done + count
    return row


PAD = 8
CPAD = 4
FAR_FIELDS, FAR_COT = 7, 5


def main_kernel(
    dims, fields_in, w_down_in, w_pool_in, w_mid_in, w_unpool_in, w_up_in, cot_in,
    out_hbm, gf_hbm, grads_hbm,
    out_s, gf_s, grads,
    raw, w_down, w_pool, w_mid, w_unpool, w_up,
    fc, sk, dd, co, dm,
    sk_send, dd_send, co_send, dm_send,
    fc_recv, sk_recv, dd_recv, co_recv, dm_recv,
    b_down, b_up, b_mid, p_mat, u_mat,
    shift, place, shift_c, place_c, order, back,
    hid, ds_down, g_skip, d_up,
    sum0, sum1, sum2, got0, got1, got2, mid0, mid1, mid2,
    in_sem, out_sem, ex_send, ex_recv, s1, r1, s2, r2, s3, r3,
):
    nx, ny, xs, ys, cf, cc, planes, scale, sizes = dims
    half, hx, hy = planes // 2, xs // 2, ys // 2
    width = planes * cf
    chunk = ROWS
    ix, iy = lax.axis_index("gx"), lax.axis_index("gy")

    def at(dx, dy):
        return {"gx": lax.rem(ix + (dx + nx), nx), "gy": lax.rem(iy + (dy + ny), ny)}

    partners = [(dx, 0) for dx in range(1, nx)] + [(0, dy) for dy in range(1, ny)]
    partners += [(dx, dy) for dx in (-1, 1) for dy in (-1, 1)]
    barrier = pltpu.get_barrier_semaphore()
    for dx, dy in partners:
        pl.semaphore_signal(barrier, inc=1, device_id=at(dx, dy), device_id_type=MESH)

    loads = {}
    for spot, (name, src, dst) in enumerate((
        ("fields", fields_in, raw.at[0]), ("cot", cot_in, raw.at[1]), ("down", w_down_in, w_down),
        ("pool", w_pool_in, w_pool), ("up", w_up_in, w_up), ("mid", w_mid_in, w_mid),
        ("unpool", w_unpool_in, w_unpool),
    )):
        loads[name] = pltpu.make_async_copy(src, dst, in_sem.at[spot])
        loads[name].start()

    def send(src, dst, ssem, rsem, dx, dy):
        copy = pltpu.make_async_remote_copy(
            src_ref=src, dst_ref=dst, send_sem=ssem, recv_sem=rsem,
            device_id=at(dx, dy), device_id_type=MESH,
        )
        copy.start()
        return copy

    def exchange(number, snd, rcv):
        ss, rs = ex_send.at[number], ex_recv.at[number]
        return [
            send(snd.at[0], rcv.at[0], ss.at[0], rs.at[0], -1, 0),
            send(snd.at[1], rcv.at[1], ss.at[1], rs.at[1], 1, 0),
        ]

    def arrive(copies):
        for copy in copies:
            copy.wait_recv()

    def lines(buf, index, first, count, start, stop):
        value = buf[index, PAD + first : PAD + first + count, :, start:stop]
        return value.reshape(count * xs, stop - start)

    def clines(buf, first, count, start, stop):
        value = buf[CPAD + first : CPAD + first + count, :, start:stop]
        return value.reshape(count * hx, stop - start).astype(BF16)

    def fine_shifts(buf, index, halo):
        for cut in range((ys + 2 * PAD) // chunk):
            span = slice(cut * chunk, (cut + 1) * chunk)
            own = buf[index, span, :, width : 2 * width].reshape(chunk * xs, width)
            both = dot(shift[...], own)
            for side, lane in ((0, 2 * width), (1, 0)):
                moved = both[side * chunk * xs : (side + 1) * chunk * xs]
                moved = moved + dot(place[side], halo(side, cut * chunk))
                buf[index, span, :, lane : lane + width] = moved.astype(BF16).reshape(
                    chunk, xs, width
                )

    def coarse_shifts(buf, rcv):
        rows = buf.shape[0]
        own = buf[:, :, width : 2 * width].reshape(rows * hx, width).astype(BF16)
        both = dot(shift_c[...], own)
        for side, lane in ((0, 2 * width), (1, 0)):
            moved = both[side * rows * hx : (side + 1) * rows * hx]
            moved = moved + dot(place_c[side], rcv[side])
            buf[:, :, lane : lane + width] = moved.reshape(rows, hx, width)

    def fine_edges(buf, snd):
        cuts = [(-2, 2, chunk - 2), (ys, 2, 0)]
        cuts += [(first, chunk, 0) for first in range(0, ys, chunk)]
        for first, count, base in cuts:
            own = lines(buf, 0, first, count, width, 2 * width)
            row = chunk + first - base
            both = dot(edge_matrix(chunk, count, xs, base), own).astype(BF16)
            for side in range(2):
                snd[side, row : row + chunk, :] = both[side * chunk : (side + 1) * chunk]

    def coarse_edges(buf, snd):
        rows, kept = buf.shape[0], snd.shape[1]
        own = buf[:, :, width : 2 * width].reshape(rows * hx, width).astype(BF16)
        both = dot(edge_matrix(kept, rows, hx, 0), own).astype(BF16)
        for side in range(2):
            snd[side] = both[side * kept : (side + 1) * kept]

    def conv(buf, index, first, count, band):
        total = None
        for bb in range(3):
            term = dot(
                lines(buf, index, first + bb - 1, count, 0, 3 * width),
                band[3 * bb : 3 * bb + 3].reshape(3 * width, width),
            )
            total = term if total is None else total + term
        return total

    def conv_t(buf, index, first, count, band):
        total = None
        for bb in range(3):
            for aa in range(3):
                left = lines(buf, index, first + bb - 1, count, aa * width, (aa + 1) * width)
                term = dot_t(left, band[3 * (2 - bb) + 2 - aa])
                total = term if total is None else total + term
        return total

    def groups(value, count, ii, jj):
        value = value.reshape(count // 2, 2, xs, width)[:, jj, ii * hx : (ii + 1) * hx]
        return value.reshape(count // 2 * hx, width).astype(BF16)

    def woven(terms, count):
        sides = [
            jnp.concatenate(
                [terms[ii][jj].reshape(count // 2, hx, width) for ii in range(2)], axis=1
            ).reshape(count // 2, 1, xs, width)
            for jj in range(2)
        ]
        return jnp.concatenate(sides, axis=1).reshape(count, xs, width)

    def frame(buf, first, count):
        return buf[PAD + first : PAD + first + count]

    order[...] = row_matrix(xs, ys)
    for buf, index, low, high in ((fc, 0, -7, ys + 7), (fc, 1, -5, ys + 5), (sk, 0, -4, ys + 4), (dd, 0, -2, ys + 2)):
        for start, stop in ((0, PAD + low), (PAD + high, buf.shape[1])):
            buf[index, start:stop, :, width : 2 * width] = jnp.zeros((stop - start, xs, width), BF16)
    for buf, low, high in ((co, -3, hy + 3), (dm, -2, hy + 2)):
        for start, stop in ((0, CPAD + low), (CPAD + high, buf.shape[0])):
            buf[start:stop, :, width : 2 * width] = jnp.zeros((stop - start, hx, width), F32)

    for index, name in ((0, "fields"), (1, "cot")):
        loads[name].wait()
        value = dot(order[...], raw[index]).astype(BF16)
        fc[index, PAD : PAD + ys, :, width : 2 * width] = value.reshape(ys, xs, width)
    pl.semaphore_wait(barrier, len(partners))
    ss, rs = ex_send.at[0], ex_recv.at[0]
    moving, spot = [], 0
    for side, dx, row in ((0, -1, 0), (1, 1, (xs - 1) * ys)):
        for dy, first, count, target in ((0, 0, ys, chunk), (-1, 0, chunk, chunk + ys),
                                         (1, ys - chunk, chunk, 0)):
            moving.append(
                send(
                    raw.at[:, row + first : row + first + count, :],
                    fc_recv.at[side, :, target : target + count, :],
                    ss.at[spot], rs.at[spot], dx, dy,
                )
            )
            spot += 1
    for index, far in ((0, FAR_FIELDS), (1, FAR_COT)):
        for dy, first, target in ((-1, 0, ys), (1, ys - far, -far)):
            moving.append(
                send(
                    fc.at[index, PAD + first : PAD + first + far, :, width : 2 * width],
                    fc.at[index, PAD + target : PAD + target + far, :, width : 2 * width],
                    ss.at[spot], rs.at[spot], 0, dy,
                )
            )
            spot += 1

    for side, step in ((0, 1), (1, -1)):
        shift[side * chunk * xs : (side + 1) * chunk * xs, :] = fine_shift(chunk, xs, step)
        place[side] = halo_matrix(chunk, xs, 2 * chunk, chunk - PAD, step)
        tall = co.shape[0] * hx
        shift_c[side * tall : (side + 1) * tall, :] = coarse_shift(co.shape[0], hx, step)
        place_c[side] = halo_matrix(co.shape[0], hx, 2 * chunk, 0, step)
    back[...] = row_matrix_back(xs, ys)
    loads["down"].wait()
    build_band(w_down, b_down, planes, cf, width)
    loads["pool"].wait()
    build_pool(w_pool, p_mat, half, cf, cc, width)
    loads["up"].wait()
    build_band(w_up, b_up, planes, cf, width)
    loads["mid"].wait()
    build_band(w_mid, b_mid, half, cc, width)

    arrive(moving)
    sends = list(moving)

    def fine_halo(rcv):
        return lambda side, cut: rcv[side, cut : cut + 2 * chunk, :]

    fine_shifts(fc, 0, lambda side, cut: fc_recv[side, 0, cut : cut + 2 * chunk, :])
    part = hy + 6
    for first in (-6, -6 + part):
        value, slope = silu_parts(conv(fc, 0, first, part, b_down))
        value = value.astype(BF16).astype(F32)
        hid[PAD + first : PAD + first + part] = value.reshape(part, xs, width)
        ds_down[PAD + first : PAD + first + part] = slope.reshape(part, xs, width)
    pre_pool = None
    for jj in range(2):
        for ii in range(2):
            term = dot(groups(frame(hid, -6, ys + 12), ys + 12, ii, jj), p_mat[2 * ii + jj])
            pre_pool = term if pre_pool is None else pre_pool + term
    coarse, ds_pool = silu_parts(pre_pool)
    coarse = coarse.astype(BF16).astype(F32)
    co[CPAD - 3 : CPAD + hy + 3, :, width : 2 * width] = coarse.reshape(hy + 6, hx, width)
    coarse_edges(co, co_send)
    moving = exchange(1, co_send, co_recv)

    loads["unpool"].wait()
    build_pool(w_unpool, u_mat, half, cf, cc, width)
    fine_shifts(fc, 1, lambda side, cut: fc_recv[side, 1, cut : cut + 2 * chunk, :])
    part = hy + 4
    for first in (-4, -4 + part):
        value = conv_t(fc, 1, first, part, b_up)
        g_skip[PAD + first : PAD + first + part] = value.reshape(part, xs, width)

    arrive(moving)
    sends += moving
    coarse_shifts(co, co_recv)
    pre_mid = None
    for bb in range(3):
        term = dot(
            clines(co, bb - 3, hy + 4, 0, 3 * width),
            b_mid[3 * bb : 3 * bb + 3].reshape(3 * width, width),
        )
        pre_mid = term if pre_mid is None else pre_mid + term
    value, ds_mid = silu_parts(pre_mid)
    own = co[CPAD - 2 : CPAD + hy + 2, :, width : 2 * width].reshape((hy + 4) * hx, width)
    middle = (own + value).astype(BF16)
    lifted = [[dot_t(middle, u_mat[2 * ii + jj]) for jj in range(2)] for ii in range(2)]
    pre_up = frame(hid, -4, ys + 8) + woven(lifted, ys + 8)
    value, slope = silu_parts(pre_up)
    sk[0, PAD - 4 : PAD + ys + 4, :, width : 2 * width] = value.astype(BF16)
    d_up[PAD - 4 : PAD + ys + 4] = (frame(g_skip, -4, ys + 8) * slope).astype(BF16).astype(F32)
    d_middle = None
    for jj in range(2):
        for ii in range(2):
            term = dot(groups(frame(d_up, -4, ys + 8), ys + 8, ii, jj), u_mat[2 * ii + jj])
            d_middle = term if d_middle is None else d_middle + term
    d_mid = (d_middle * ds_mid).astype(BF16)
    dm[CPAD - 2 : CPAD + hy + 2, :, width : 2 * width] = d_mid.astype(F32).reshape(
        hy + 4, hx, width
    )
    coarse_edges(dm, dm_send)
    moving = exchange(2, dm_send, dm_recv)
    fine_edges(sk, sk_send)
    skips = exchange(3, sk_send, sk_recv)

    class Reduction:
        def __init__(self, group, terms, got, mids, base):
            self.group, self.terms, self.got, self.mids, self.base = group, terms, got, mids, base
            self.rows = sizes[group] // nx

        def piece(self, index):
            return pl.ds(pl.multiple_of(index * self.rows, ROWS), self.rows)

        def scatter(self):
            self.copies = []
            for dx in range(1, nx):
                target = at(dx, 0)["gx"]
                self.copies.append(
                    send(
                        self.terms.at[self.piece(target), :], self.got.at[dx - 1],
                        s1.at[self.group, dx - 1], r1.at[self.group, dx - 1], dx, 0,
                    )
                )
            return self.copies

        def across(self):
            arrive(self.copies)
            total = self.terms[self.piece(ix), :].astype(F32)
            for dx in range(1, nx):
                total = total + self.got[dx - 1].astype(F32)
            self.mids[iy] = total.astype(BF16)
            self.copies = []
            for dy in range(1, ny):
                self.copies.append(
                    send(
                        self.mids.at[iy], self.mids.at[iy],
                        s2.at[self.group, dy - 1], r2.at[self.group, dy - 1], 0, dy,
                    )
                )
            return self.copies

        def gather(self):
            arrive(self.copies)
            total = self.mids[0].astype(F32)
            for yy in range(1, ny):
                total = total + self.mids[yy].astype(F32)
            start = pl.multiple_of(self.base + ix * self.rows, ROWS)
            mine = pl.ds(start, self.rows)
            grads[mine, :] = (total * scale).astype(BF16)
            self.copies = []
            for dx in range(1, nx):
                self.copies.append(
                    send(
                        grads.at[mine, :], grads.at[mine, :],
                        s3.at[self.group, dx - 1], r3.at[self.group, dx - 1], dx, 0,
                    )
                )
            return self.copies

    def padded_tail(ref, row, group):
        if row < sizes[group]:
            ref[row:, :] = jnp.zeros((sizes[group] - row, LANES), BF16)

    cuts = range(0, ys, chunk)

    def fine_tap(buf, index, cut, aa, bb):
        return lines(buf, index, cut * chunk + bb - 1, chunk, aa * width, (aa + 1) * width)

    own_mid = d_mid.astype(F32).reshape(hy + 4, hx, width)[2 : hy + 2].reshape(hy * hx, width)
    row = conv_grad(
        [turned(own_mid)],
        lambda index, aa, bb: clines(co, bb - 1, hy, aa * width, (aa + 1) * width),
        half, cc, width, Packer(sum0, 0, cc),
    )
    padded_tail(sum0, row, 0)
    red0 = Reduction(0, sum0, got0, mid0, 0)
    sends += red0.scatter()
    row = conv_grad(
        [turned(lines(sk, 0, first, chunk, width, 2 * width)) for first in cuts],
        lambda cut, aa, bb: fine_tap(fc, 1, cut, 2 - aa, 2 - bb),
        planes, cf, width, Packer(sum1, 0, cf), -1,
    )
    own_middle = middle.astype(F32).reshape(hy + 4, hx, width)[2 : hy + 2].reshape(hy * hx, width)
    row = pair_grad(
        turned(own_middle),
        [groups(frame(d_up, 0, ys), ys, ii, jj) for ii in range(2) for jj in range(2)],
        half, cc, width, Packer(sum1, row, cc),
    )
    padded_tail(sum1, row, 1)
    red1 = Reduction(1, sum1, got1, mid1, sizes[0])
    sends += red1.scatter()

    arrive(moving)
    sends += moving
    coarse_shifts(dm, dm_recv)
    total = None
    for bb in range(3):
        for aa in range(3):
            left = clines(dm, bb - 2, hy + 2, aa * width, (aa + 1) * width)
            term = dot_t(left, b_mid[3 * (2 - bb) + 2 - aa])
            total = term if total is None else total + term
    d_coarse = d_middle.reshape(hy + 4, hx, width)[1 : hy + 3].reshape((hy + 2) * hx, width)
    d_coarse = d_coarse + total
    slope = ds_pool.reshape(hy + 6, hx, width)[2 : hy + 4].reshape((hy + 2) * hx, width)
    d_pool = (d_coarse * slope).astype(BF16)
    backs = [[dot_t(d_pool, p_mat[2 * ii + jj]) for jj in range(2)] for ii in range(2)]
    d_hidden = frame(d_up, -2, ys + 4) + woven(backs, ys + 4)
    d_down = (d_hidden * frame(ds_down, -2, ys + 4)).astype(BF16)
    dd[0, PAD - 2 : PAD + ys + 2, :, width : 2 * width] = d_down

    row = conv_grad(
        [turned(lines(dd, 0, first, chunk, width, 2 * width)) for first in cuts],
        lambda cut, aa, bb: fine_tap(fc, 0, cut, aa, bb),
        planes, cf, width, Packer(sum2, 0, cf),
    )
    own_pool = d_pool.astype(F32).reshape(hy + 2, hx, width)[1 : hy + 1].reshape(hy * hx, width)
    row = pair_grad(
        turned(own_pool),
        [groups(frame(hid, 0, ys), ys, ii, jj) for ii in range(2) for jj in range(2)],
        half, cc, width, Packer(sum2, row, cc),
    )
    padded_tail(sum2, row, 2)
    red2 = Reduction(2, sum2, got2, mid2, sizes[0] + sizes[1])
    sends += red2.scatter()
    fine_edges(dd, dd_send)
    moving = exchange(4, dd_send, dd_recv)
    sends += red0.across()
    sends += red1.across()

    def finish(buf, index, rcv, value_of, target):
        fine_shifts(buf, 0, fine_halo(rcv))
        for first in cuts:
            own = lines(fc, index, first, chunk, width, 2 * width).astype(F32)
            hid[PAD + first : PAD + first + chunk] = (
                (own + value_of(first)).astype(BF16).astype(F32).reshape(chunk, xs, width)
            )
        value = frame(hid, 0, ys).reshape(ys * xs, width).astype(BF16)
        target[...] = dot(back[...], value).astype(BF16)

    arrive(skips)
    sends += skips
    finish(sk, 0, sk_recv, lambda first: conv(sk, 0, first, chunk, b_up), out_s)
    stores = []

    def store(src, dst):
        copy = pltpu.make_async_copy(src, dst, out_sem.at[len(stores)])
        copy.start()
        stores.append(copy)

    store(out_s, out_hbm)
    sends += red2.across()
    arrive(moving)
    sends += moving
    finish(dd, 1, dd_recv, lambda first: conv_t(dd, 0, first, chunk, b_down), gf_s)
    store(gf_s, gf_hbm)
    sends += red0.gather()
    sends += red1.gather()
    sends += red2.gather()
    for red in (red0, red1, red2):
        arrive(red.copies)
        rows = pl.ds(red.base, sizes[red.group])
        store(grads.at[rows, :], grads_hbm.at[rows, :])
    for copy in sends:
        copy.wait_send()
    for copy in stores:
        copy.wait()


def last_kernel(
    dims, out_in, gf_in, grads_in, output, grad_fields, g_down, g_pool, g_mid, g_unpool, g_up,
    st_out, st_gf, grads, st_down, st_pool, st_mid, st_unpool, st_up, in_sem, out_sem,
):
    nx, ny, xs, ys, cf, cc, planes, scale, sizes = dims
    loads = [
        pltpu.make_async_copy(src, dst, in_sem.at[spot])
        for spot, (src, dst) in enumerate(((grads_in, grads), (out_in, st_out), (gf_in, st_gf)))
    ]
    for load in loads:
        load.start()
    stores = []

    def store(src, dst):
        copy = pltpu.make_async_copy(src, dst, out_sem.at[len(stores)])
        copy.start()
        stores.append(copy)

    loads[0].wait()
    turned_blocks(grads, 0, cc, st_mid)
    store(st_mid, g_mid)
    loads[1].wait()
    store(st_out, output)
    loads[2].wait()
    store(st_gf, grad_fields)
    row = sizes[0]
    for block in range(st_up.shape[0] // cf):
        first = block * cf
        spot = block % (LANES // cf)
        if spot == 0:
            held = grads[row : row + cf, :].astype(F32)
            row += cf
        moved = held if spot == 0 else pltpu.roll(held, LANES - spot * cf, 1)
        st_up[first : first + cf, :] = moved[:, :cf]
    store(st_up, g_up)
    turned_blocks(grads, row, cc, st_unpool)
    store(st_unpool, g_unpool)
    row = turned_blocks(grads, sizes[0] + sizes[1], cf, st_down)
    store(st_down, g_down)
    turned_blocks(grads, row, cc, st_pool)
    store(st_pool, g_pool)
    for copy in stores:
        copy.wait()


def per_device(dims, fields, w_down, w_pool, w_mid, w_unpool, w_up, cotangent):
    nx, ny, xs, ys, cf, cc, planes, scale, sizes = dims
    hx, hy = xs // 2, ys // 2
    width = planes * cf
    hbm = pl.BlockSpec(memory_space=pl.ANY)
    tall, tall_c = ys + 2 * PAD, hy + 2 * CPAD

    def fine(lead=1):
        return pltpu.VMEM((lead, tall, xs, 3 * width), BF16)

    def coarse():
        return pltpu.VMEM((tall_c, hx, 3 * width), F32)

    def line(*shape):
        return pltpu.VMEM((2,) + shape + (width,), BF16)

    def sems(*shape):
        return pltpu.SemaphoreType.DMA(shape)

    def f32(*shape):
        return jax.ShapeDtypeStruct(shape, F32)

    def stage(values):
        return [pltpu.VMEM(value.shape, value.dtype) for value in values]

    rows = [size // nx for size in sizes]
    flat = jax.ShapeDtypeStruct((xs * ys, width), BF16)
    kept = ys + 2 * ROWS
    weights = (
        w_down.reshape(-1, cf),
        w_pool.reshape(-1, cc),
        w_mid.reshape(-1, cc),
        jnp.swapaxes(w_unpool, 3, 4).reshape(-1, cc),
        w_up.reshape(-1, cf),
    )
    total = jax.ShapeDtypeStruct((sum(sizes), LANES), BF16)
    mains = pl.pallas_call(
        functools.partial(main_kernel, dims),
        out_shape=(flat, flat, total),
        in_specs=[hbm] * 7,
        out_specs=(hbm,) * 3,
        scratch_shapes=[
            *stage((flat, flat, total)),
            pltpu.VMEM((2, xs * ys, width), BF16),
            *stage(weights),
            fine(2), fine(), fine(), coarse(), coarse(),
            line(kept), line(kept), line(2 * ROWS), line(2 * ROWS),
            line(2, kept), line(kept), line(kept), line(2 * ROWS), line(2 * ROWS),
            pltpu.VMEM((9, width, width), BF16),
            pltpu.VMEM((9, width, width), BF16),
            pltpu.VMEM((9, width, width), BF16),
            pltpu.VMEM((4, width, width), BF16),
            pltpu.VMEM((4, width, width), BF16),
            pltpu.VMEM((2 * ROWS * xs, ROWS * xs), BF16),
            pltpu.VMEM((2, ROWS * xs, 2 * ROWS), BF16),
            pltpu.VMEM((2 * tall_c * hx, tall_c * hx), BF16),
            pltpu.VMEM((2, tall_c * hx, 2 * ROWS), BF16),
            pltpu.VMEM((xs * ys, xs * ys), BF16),
            pltpu.VMEM((xs * ys, xs * ys), BF16),
            *[pltpu.VMEM((tall, xs, width), F32) for _ in range(4)],
            *[pltpu.VMEM((size, LANES), BF16) for size in sizes],
            *[pltpu.VMEM((nx - 1, row, LANES), BF16) for row in rows],
            *[pltpu.VMEM((ny, row, LANES), BF16) for row in rows],
            sems(7), sems(5),
            sems(5, 10), sems(5, 10),
            sems(3, nx - 1), sems(3, nx - 1),
            sems(3, ny - 1), sems(3, ny - 1),
            sems(3, nx - 1), sems(3, nx - 1),
        ],
        compiler_params=pltpu.CompilerParams(
            collective_id=0, has_side_effects=True, vmem_limit_bytes=60 << 20
        ),
        name="unet",
    )(fields.reshape(xs * ys, width), *weights, cotangent.reshape(xs * ys, width))

    results = (
        flat, flat, f32(27 * cf, cf), f32(8 * cf, cc), f32(27 * cc, cc), f32(8 * cf, cc),
        f32(27 * cf, cf),
    )
    output, grad_fields, g_down, g_pool, g_mid, g_unpool, g_up = pl.pallas_call(
        functools.partial(last_kernel, dims),
        out_shape=results,
        in_specs=[hbm] * 3,
        out_specs=(hbm,) * 7,
        scratch_shapes=[*stage((flat, flat, total)), *stage(results[2:]), sems(3), sems(7)],
        name="layouts",
    )(*mains)
    swapped = w_unpool.shape[:3] + (cf, cc)
    return (
        output.reshape(fields.shape),
        grad_fields.reshape(fields.shape),
        g_down.reshape(w_down.shape),
        g_pool.reshape(w_pool.shape),
        g_mid.reshape(w_mid.shape),
        jnp.swapaxes(g_unpool.reshape(swapped), 3, 4),
        g_up.reshape(w_up.shape),
    )


def solution(mesh):
    nx, ny = mesh.shape["gx"], mesh.shape["gy"]

    def whole(fields, w_down, w_pool, w_mid, w_unpool, w_up, cotangent):
        cf, cc = w_down.shape[3], w_mid.shape[3]
        xs, ys = fields.shape[0] // nx, fields.shape[1] // ny
        planes = fields.shape[2] // cf
        scale = 1.0 / math.sqrt(fields.shape[0] * fields.shape[1] * planes)

        def blocks(taps, chan):
            return -(-taps * chan // LANES) * chan

        fine_rows = blocks(27, cf)
        pair_rows = 4 * cc * 2 * cf // LANES
        unit = ROWS * nx
        sizes = tuple(
            -(-rows // unit) * unit
            for rows in (blocks(27, cc), fine_rows + pair_rows, fine_rows + pair_rows)
        )
        dims = (nx, ny, xs, ys, cf, cc, planes, scale, sizes)
        placed = (P("gx", "gy", None), P(), P(), P(), P(), P(), P("gx", "gy", None))
        return jax.shard_map(
            functools.partial(per_device, dims),
            mesh=mesh,
            in_specs=placed,
            out_specs=(P("gx", "gy", None), P("gx", "gy", None), P(), P(), P(), P(), P()),
            check_vma=False,
        )(fields, w_down, w_pool, w_mid, w_unpool, w_up, cotangent)

    return whole
```

```python
import functools
import math

import jax
import jax.numpy as jnp
from jax import lax
from jax.experimental import pallas as pl
from jax.experimental.pallas import tpu as pltpu
from jax.sharding import PartitionSpec as P

BF16 = jnp.bfloat16
F32 = jnp.float32
MESH = pl.DeviceIdType.MESH
LANES = 128
ROWS = 16


def dot(left, right):
    return lax.dot_general(left, right, (((1,), (0,)), ((), ())), preferred_element_type=F32)


def dot_t(left, right):
    return lax.dot_general(left, right, (((1,), (1,)), ((), ())), preferred_element_type=F32)


def iota(shape, dim):
    return lax.broadcasted_iota(jnp.int32, shape, dim)


def div(value, by):
    if by & (by - 1) == 0:
        return lax.shift_right_logical(value, jnp.int32(by.bit_length() - 1))
    return lax.div(value, jnp.int32(by))


def rem(value, by):
    if by & (by - 1) == 0:
        return value & jnp.int32(by - 1)
    return lax.rem(value, jnp.int32(by))


def row_col(shape):
    return iota((shape[0], 1), 0), iota((1, shape[1]), 1)


def one_hot(mask):
    return jnp.where(mask, 1.0, 0.0).astype(BF16)


def silu_parts(value):
    sig = jax.nn.sigmoid(value)
    return value * sig, sig * (1.0 + value * (1.0 - sig))


def row_matrix(xs, ys):
    hx = xs // 2
    shape = (xs * ys, xs * ys)
    row, col = row_col(shape)
    place = rem(row, xs)
    across = rem(place, hx) * 2 + div(place, hx)
    return one_hot(col == across * ys + div(row, xs))


def row_matrix_back(xs, ys):
    hx = xs // 2
    shape = (xs * ys, xs * ys)
    row, col = row_col(shape)
    across = div(row, ys)
    return one_hot(col == rem(row, ys) * xs + rem(across, 2) * hx + div(across, 2))


def fine_shift(lines, xs, step):
    hx = xs // 2
    shape = (lines * xs, lines * xs)
    row, col = row_col(shape)
    place = rem(row, xs)
    first = place < hx
    if step > 0:
        wanted = jnp.where(first, row + hx, row - hx + 1)
        edge = xs - 1
    else:
        wanted = jnp.where(first, row + hx - 1, row - hx)
        edge = 0
    return one_hot((col == wanted) & (place != edge))


def coarse_shift(lines, hx, step):
    shape = (lines * hx, lines * hx)
    row, col = row_col(shape)
    edge = hx - 1 if step > 0 else 0
    return one_hot((col == row + step) & (rem(row, hx) != edge))


def halo_matrix(lines, across, depth, base, step):
    shape = (lines * across, depth)
    row, col = row_col(shape)
    edge = across - 1 if step > 0 else 0
    return one_hot((rem(row, across) == edge) & (col == div(row, across) + base))


def edge_matrix(rows, lines, across, base):
    shape = (2 * rows, lines * across)
    row, col = row_col(shape)
    first = row < rows
    line = jnp.where(first, row, row - rows) - base
    return one_hot(col == line * across + jnp.where(first, 0, across - 1))


def tile_matrix(small, width):
    shape = (small, width)
    row, col = row_col(shape)
    return one_hot(rem(col, small) == row)


def build_band(weight, band, planes, chan, width):
    tile = tile_matrix(chan, width)
    plane = div(iota((chan, width), 1), chan)

    def step(tap, carry):
        start = pl.multiple_of(tap * (3 * chan), ROWS)
        wide = dot(weight[pl.ds(start, 3 * chan), :], tile)
        spot = rem(tap, 3) * 3 + div(tap, 3)
        parts = [wide[kk * chan : (kk + 1) * chan] for kk in range(3)]
        for pp in range(planes):
            block = jnp.zeros((chan, width), F32)
            for kk in range(3):
                block = jnp.where(plane == pp + 1 - kk, parts[kk], block)
            band[spot, pp * chan : (pp + 1) * chan, :] = block.astype(BF16)
        return carry

    lax.fori_loop(0, 9, step, 0)


def build_pool(weight, mats, half, cf, cc, width):
    wide = dot(weight[...], tile_matrix(cc, width))
    plane = div(iota((2 * cf, width), 1), cc)
    for ij in range(4):
        part = wide[ij * 2 * cf : (ij + 1) * 2 * cf]
        for zz in range(half):
            block = jnp.where(plane == zz, part, 0.0)
            mats[ij, zz * 2 * cf : (zz + 1) * 2 * cf, :] = block.astype(BF16)


def folded(block, chan):
    total = block[:, :LANES]
    for part in range(1, block.shape[1] // LANES):
        total = total + block[:, part * LANES : (part + 1) * LANES]
    step = LANES // 2
    while step >= chan:
        total = total + pltpu.roll(total, step, 1)
        step //= 2
    return total


class Packer:
    def __init__(self, target, row, chan):
        self.target, self.row, self.chan = target, row, chan
        self.per = LANES // chan
        self.group = div(iota((chan, LANES), 1), chan)
        self.held, self.count = None, 0

    def add(self, value):
        spot = self.count % self.per
        self.held = value if spot == 0 else jnp.where(self.group == spot, value, self.held)
        self.count += 1
        if spot == self.per - 1:
            self.flush()

    def flush(self):
        if self.held is not None:
            self.target[self.row : self.row + self.chan, :] = self.held.astype(BF16)
            self.row += self.chan
            self.held = None
        return self.row


def conv_grad(parts, tap_of, planes, chan, width, packer, sign=1):
    plane = div(iota((chan, width), 1), chan)
    for tap in range(9):
        dband = None
        for index, part in enumerate(parts):
            term = dot(part, tap_of(index, tap // 3, tap % 3))
            dband = term if dband is None else dband + term
        for kk in range(3):
            total = jnp.zeros((chan, width), F32)
            for zz in range(planes):
                lane = zz + sign * (kk - 1)
                if 0 <= lane < planes:
                    rows = dband[zz * chan : (zz + 1) * chan]
                    total = jnp.where(plane == lane, rows, total)
            packer.add(folded(total, chan))
    return packer.flush()


def pair_grad(left_t, rights, half, chan, width, packer):
    plane = div(iota((chan, width), 1), width // half)
    for right in rights:
        full = dot(left_t, right)
        total = jnp.zeros((chan, width), F32)
        for zz in range(half):
            total = jnp.where(plane == zz, full[zz * chan : (zz + 1) * chan], total)
        packer.add(folded(total, width // half))
    return packer.flush()


def turned(value):
    return value.astype(F32).T.astype(BF16)


def turned_blocks(source, row, chan, target):
    done, total = 0, target.shape[0]
    while done < total:
        block = source[row : row + chan, :].astype(F32).T
        count = min(LANES, total - done)
        target[done : done + count, :] = block[:count]
        row, done = row + chan, done + count
    return row


PAD = 8
CPAD = 4
FAR_FIELDS, FAR_COT = 5, 3


def main_kernel(
    dims, fields_in, w_down_in, w_pool_in, w_mid_in, w_unpool_in, w_up_in, cot_in,
    out_hbm, gf_hbm, grads_hbm,
    out_s, gf_s, grads,
    raw, w_down, w_pool, w_mid, w_unpool, w_up,
    fc, sk, dd, co, dm,
    sk_send, dd_send, co_send, dm_send,
    fc_recv, sk_recv, dd_recv, co_recv, dm_recv,
    b_down, b_up, b_mid, p_mat, u_mat,
    shift, place, shift_c, place_c, order, back,
    hid, ds_down, g_skip, d_up,
    sum0, sum1, sum2, got0, got1, got2, mid0, mid1, mid2,
    in_sem, out_sem, ex_send, ex_recv, s1, r1, s2, r2, s3, r3,
):
    nx, ny, xs, ys, cf, cc, planes, scale, sizes = dims
    half, hx, hy = planes // 2, xs // 2, ys // 2
    width = planes * cf
    chunk = ROWS
    ix, iy = lax.axis_index("gx"), lax.axis_index("gy")

    def at(dx, dy):
        return {"gx": lax.rem(ix + (dx + nx), nx), "gy": lax.rem(iy + (dy + ny), ny)}

    partners = [(dx, 0) for dx in range(1, nx)] + [(0, dy) for dy in range(1, ny)]
    partners += [(dx, dy) for dx in (-1, 1) for dy in (-1, 1)]
    barrier = pltpu.get_barrier_semaphore()
    for dx, dy in partners:
        pl.semaphore_signal(barrier, inc=1, device_id=at(dx, dy), device_id_type=MESH)

    loads = {}
    for spot, (name, src, dst) in enumerate((
        ("fields", fields_in, raw.at[0]), ("cot", cot_in, raw.at[1]), ("down", w_down_in, w_down),
        ("pool", w_pool_in, w_pool), ("up", w_up_in, w_up), ("mid", w_mid_in, w_mid),
        ("unpool", w_unpool_in, w_unpool),
    )):
        loads[name] = pltpu.make_async_copy(src, dst, in_sem.at[spot])
        loads[name].start()

    def send(src, dst, ssem, rsem, dx, dy):
        copy = pltpu.make_async_remote_copy(
            src_ref=src, dst_ref=dst, send_sem=ssem, recv_sem=rsem,
            device_id=at(dx, dy), device_id_type=MESH,
        )
        copy.start()
        return copy

    def exchange(number, snd, rcv):
        ss, rs = ex_send.at[number], ex_recv.at[number]
        return [
            send(snd.at[0], rcv.at[0], ss.at[0], rs.at[0], -1, 0),
            send(snd.at[1], rcv.at[1], ss.at[1], rs.at[1], 1, 0),
        ]

    def around(number, snd, rcv, start):
        ss, rs = ex_send.at[number], ex_recv.at[number]
        copies, spot = [], 0
        for side, dx in ((0, -1), (1, 1)):
            for dy, first, count, target in ((0, 0, ys, chunk), (-1, 0, chunk, chunk + ys),
                                             (1, ys - chunk, chunk, 0)):
                if start is None:
                    src = snd[side].at[:, first : first + count, :]
                    dst = rcv[side].at[:, target : target + count, :]
                else:
                    first = first + chunk
                    src = snd.at[side, first : first + count, :]
                    dst = rcv.at[side, target : target + count, :]
                copies.append(send(src, dst, ss.at[spot], rs.at[spot], dx, dy))
                spot += 1
        return copies

    def arrive(copies):
        for copy in copies:
            copy.wait_recv()

    def lines(buf, index, first, count, start, stop):
        value = buf[index, PAD + first : PAD + first + count, :, start:stop]
        return value.reshape(count * xs, stop - start)

    def clines(buf, first, count, start, stop):
        value = buf[CPAD + first : CPAD + first + count, :, start:stop]
        return value.reshape(count * hx, stop - start).astype(BF16)

    def fine_shifts(buf, index, halo):
        for cut in range((ys + 2 * PAD) // chunk):
            span = slice(cut * chunk, (cut + 1) * chunk)
            own = buf[index, span, :, width : 2 * width].reshape(chunk * xs, width)
            both = dot(shift[...], own)
            for side, lane in ((0, 2 * width), (1, 0)):
                moved = both[side * chunk * xs : (side + 1) * chunk * xs]
                moved = moved + dot(place[side], halo(side, cut * chunk))
                buf[index, span, :, lane : lane + width] = moved.astype(BF16).reshape(
                    chunk, xs, width
                )

    def coarse_shifts(buf, rcv):
        rows = buf.shape[0]
        own = buf[:, :, width : 2 * width].reshape(rows * hx, width).astype(BF16)
        both = dot(shift_c[...], own)
        for side, lane in ((0, 2 * width), (1, 0)):
            moved = both[side * rows * hx : (side + 1) * rows * hx]
            moved = moved + dot(place_c[side], rcv[side])
            buf[:, :, lane : lane + width] = moved.reshape(rows, hx, width)

    def fine_edges(buf, snd, outer):
        cuts = [(-2, 2, chunk - 2), (ys, 2, 0)] if outer else []
        cuts += [(first, chunk, 0) for first in range(0, ys, chunk)]
        for first, count, base in cuts:
            own = lines(buf, 0, first, count, width, 2 * width)
            row = chunk + first - base
            both = dot(edge_matrix(chunk, count, xs, base), own).astype(BF16)
            for side in range(2):
                snd[side, row : row + chunk, :] = both[side * chunk : (side + 1) * chunk]

    def coarse_edges(buf, snd):
        rows, kept = buf.shape[0], snd.shape[1]
        own = buf[:, :, width : 2 * width].reshape(rows * hx, width).astype(BF16)
        both = dot(edge_matrix(kept, rows, hx, 0), own).astype(BF16)
        for side in range(2):
            snd[side] = both[side * kept : (side + 1) * kept]

    def conv(buf, index, first, count, band):
        total = None
        for bb in range(3):
            term = dot(
                lines(buf, index, first + bb - 1, count, 0, 3 * width),
                band[3 * bb : 3 * bb + 3].reshape(3 * width, width),
            )
            total = term if total is None else total + term
        return total

    def conv_t(buf, index, first, count, band):
        total = None
        for bb in range(3):
            for aa in range(3):
                left = lines(buf, index, first + bb - 1, count, aa * width, (aa + 1) * width)
                term = dot_t(left, band[3 * (2 - bb) + 2 - aa])
                total = term if total is None else total + term
        return total

    def groups(value, count, ii, jj):
        value = value.reshape(count // 2, 2, xs, width)[:, jj, ii * hx : (ii + 1) * hx]
        return value.reshape(count // 2 * hx, width).astype(BF16)

    def woven(terms, count):
        sides = [
            jnp.concatenate(
                [terms[ii][jj].reshape(count // 2, hx, width) for ii in range(2)], axis=1
            ).reshape(count // 2, 1, xs, width)
            for jj in range(2)
        ]
        return jnp.concatenate(sides, axis=1).reshape(count, xs, width)

    def frame(buf, first, count):
        return buf[PAD + first : PAD + first + count]

    order[...] = row_matrix(xs, ys)
    for buf, index, low, high in ((fc, 0, -5, ys + 5), (fc, 1, -3, ys + 3), (sk, 0, -2, ys + 2), (dd, 0, -1, ys + 1)):
        for start, stop in ((0, PAD + low), (PAD + high, buf.shape[1])):
            buf[index, start:stop, :, width : 2 * width] = jnp.zeros((stop - start, xs, width), BF16)
    for buf, low, high in ((co, -2, hy + 2), (dm, -1, hy + 1)):
        for start, stop in ((0, CPAD + low), (CPAD + high, buf.shape[0])):
            buf[start:stop, :, width : 2 * width] = jnp.zeros((stop - start, hx, width), F32)

    for index, name in ((0, "fields"), (1, "cot")):
        loads[name].wait()
        value = dot(order[...], raw[index]).astype(BF16)
        fc[index, PAD : PAD + ys, :, width : 2 * width] = value.reshape(ys, xs, width)
    pl.semaphore_wait(barrier, len(partners))
    rows = tuple(raw.at[:, row : row + ys, :] for row in (0, (xs - 1) * ys))
    moving = around(0, rows, tuple(fc_recv.at[side] for side in range(2)), None)

    def far_lines(index, far, spot):
        copies = []
        for dy, first, target in ((-1, 0, ys), (1, ys - far, -far)):
            copies.append(
                send(
                    fc.at[index, PAD + first : PAD + first + far, :, width : 2 * width],
                    fc.at[index, PAD + target : PAD + target + far, :, width : 2 * width],
                    ex_send.at[0, spot], ex_recv.at[0, spot], 0, dy,
                )
            )
            spot += 1
        return copies

    moving += far_lines(0, FAR_FIELDS, 6)

    for side, step in ((0, 1), (1, -1)):
        shift[side * chunk * xs : (side + 1) * chunk * xs, :] = fine_shift(chunk, xs, step)
        place[side] = halo_matrix(chunk, xs, 2 * chunk, chunk - PAD, step)
        tall = co.shape[0] * hx
        shift_c[side * tall : (side + 1) * tall, :] = coarse_shift(co.shape[0], hx, step)
        place_c[side] = halo_matrix(co.shape[0], hx, 2 * chunk, 0, step)
    back[...] = row_matrix_back(xs, ys)
    loads["down"].wait()
    build_band(w_down, b_down, planes, cf, width)
    loads["pool"].wait()
    build_pool(w_pool, p_mat, half, cf, cc, width)
    far_cot = far_lines(1, FAR_COT, 8)
    loads["up"].wait()
    build_band(w_up, b_up, planes, cf, width)
    loads["mid"].wait()
    build_band(w_mid, b_mid, half, cc, width)

    arrive(moving)
    sends = list(moving)

    def fine_halo(rcv):
        return lambda side, cut: rcv[side, cut : cut + 2 * chunk, :]

    fine_shifts(fc, 0, lambda side, cut: fc_recv[side, 0, cut : cut + 2 * chunk, :])
    part = hy + 4
    for first in (-4, -4 + part):
        value, slope = silu_parts(conv(fc, 0, first, part, b_down))
        value = value.astype(BF16).astype(F32)
        hid[PAD + first : PAD + first + part] = value.reshape(part, xs, width)
        ds_down[PAD + first : PAD + first + part] = slope.reshape(part, xs, width)
    pre_pool = None
    for jj in range(2):
        for ii in range(2):
            term = dot(groups(frame(hid, -4, ys + 8), ys + 8, ii, jj), p_mat[2 * ii + jj])
            pre_pool = term if pre_pool is None else pre_pool + term
    coarse, ds_pool = silu_parts(pre_pool)
    coarse = coarse.astype(BF16).astype(F32)
    co[CPAD - 2 : CPAD + hy + 2, :, width : 2 * width] = coarse.reshape(hy + 4, hx, width)
    coarse_edges(co, co_send)
    moving = exchange(1, co_send, co_recv)

    loads["unpool"].wait()
    build_pool(w_unpool, u_mat, half, cf, cc, width)
    arrive(far_cot)
    sends += far_cot
    fine_shifts(fc, 1, lambda side, cut: fc_recv[side, 1, cut : cut + 2 * chunk, :])
    part = hy + 2
    for first in (-2, -2 + part):
        value = conv_t(fc, 1, first, part, b_up)
        g_skip[PAD + first : PAD + first + part] = value.reshape(part, xs, width)

    arrive(moving)
    sends += moving
    coarse_shifts(co, co_recv)
    pre_mid = None
    for bb in range(3):
        term = dot(
            clines(co, bb - 2, hy + 2, 0, 3 * width),
            b_mid[3 * bb : 3 * bb + 3].reshape(3 * width, width),
        )
        pre_mid = term if pre_mid is None else pre_mid + term
    value, ds_mid = silu_parts(pre_mid)
    own = co[CPAD - 1 : CPAD + hy + 1, :, width : 2 * width].reshape((hy + 2) * hx, width)
    middle = (own + value).astype(BF16)
    lifted = [[dot_t(middle, u_mat[2 * ii + jj]) for jj in range(2)] for ii in range(2)]
    pre_up = frame(hid, -2, ys + 4) + woven(lifted, ys + 4)
    value, slope = silu_parts(pre_up)
    sk[0, PAD - 2 : PAD + ys + 2, :, width : 2 * width] = value.astype(BF16)
    d_up[PAD - 2 : PAD + ys + 2] = (frame(g_skip, -2, ys + 4) * slope).astype(BF16).astype(F32)
    d_middle = None
    for jj in range(2):
        for ii in range(2):
            term = dot(groups(frame(d_up, -2, ys + 4), ys + 4, ii, jj), u_mat[2 * ii + jj])
            d_middle = term if d_middle is None else d_middle + term
    d_mid = (d_middle * ds_mid).astype(BF16)
    dm[CPAD - 1 : CPAD + hy + 1, :, width : 2 * width] = d_mid.astype(F32).reshape(
        hy + 2, hx, width
    )
    coarse_edges(dm, dm_send)
    moving = exchange(2, dm_send, dm_recv)
    fine_edges(sk, sk_send, True)
    skips = exchange(3, sk_send, sk_recv)

    class Reduction:
        def __init__(self, group, terms, got, mids, base):
            self.group, self.terms, self.got, self.mids, self.base = group, terms, got, mids, base
            self.rows = sizes[group] // nx

        def piece(self, index):
            return pl.ds(pl.multiple_of(index * self.rows, ROWS), self.rows)

        def scatter(self):
            self.copies = []
            for dx in range(1, nx):
                target = at(dx, 0)["gx"]
                self.copies.append(
                    send(
                        self.terms.at[self.piece(target), :], self.got.at[dx - 1],
                        s1.at[self.group, dx - 1], r1.at[self.group, dx - 1], dx, 0,
                    )
                )
            return self.copies

        def across(self):
            arrive(self.copies)
            total = self.terms[self.piece(ix), :].astype(F32)
            for dx in range(1, nx):
                total = total + self.got[dx - 1].astype(F32)
            self.mids[iy] = total.astype(BF16)
            self.copies = []
            for dy in range(1, ny):
                self.copies.append(
                    send(
                        self.mids.at[iy], self.mids.at[iy],
                        s2.at[self.group, dy - 1], r2.at[self.group, dy - 1], 0, dy,
                    )
                )
            return self.copies

        def gather(self):
            arrive(self.copies)
            total = self.mids[0].astype(F32)
            for yy in range(1, ny):
                total = total + self.mids[yy].astype(F32)
            start = pl.multiple_of(self.base + ix * self.rows, ROWS)
            mine = pl.ds(start, self.rows)
            grads[mine, :] = (total * scale).astype(BF16)
            self.copies = []
            for dx in range(1, nx):
                self.copies.append(
                    send(
                        grads.at[mine, :], grads.at[mine, :],
                        s3.at[self.group, dx - 1], r3.at[self.group, dx - 1], dx, 0,
                    )
                )
            return self.copies

    def padded_tail(ref, row, group):
        if row < sizes[group]:
            ref[row:, :] = jnp.zeros((sizes[group] - row, LANES), BF16)

    cuts = range(0, ys, chunk)

    def fine_tap(buf, index, cut, aa, bb):
        return lines(buf, index, cut * chunk + bb - 1, chunk, aa * width, (aa + 1) * width)

    own_mid = d_mid.astype(F32).reshape(hy + 2, hx, width)[1 : hy + 1].reshape(hy * hx, width)
    row = conv_grad(
        [turned(own_mid)],
        lambda index, aa, bb: clines(co, bb - 1, hy, aa * width, (aa + 1) * width),
        half, cc, width, Packer(sum0, 0, cc),
    )
    padded_tail(sum0, row, 0)
    red0 = Reduction(0, sum0, got0, mid0, 0)
    sends += red0.scatter()
    row = conv_grad(
        [turned(lines(sk, 0, first, chunk, width, 2 * width)) for first in cuts],
        lambda cut, aa, bb: fine_tap(fc, 1, cut, 2 - aa, 2 - bb),
        planes, cf, width, Packer(sum1, 0, cf), -1,
    )
    own_middle = middle.astype(F32).reshape(hy + 2, hx, width)[1 : hy + 1].reshape(hy * hx, width)
    row = pair_grad(
        turned(own_middle),
        [groups(frame(d_up, 0, ys), ys, ii, jj) for ii in range(2) for jj in range(2)],
        half, cc, width, Packer(sum1, row, cc),
    )
    padded_tail(sum1, row, 1)
    red1 = Reduction(1, sum1, got1, mid1, sizes[0])
    sends += red1.scatter()

    arrive(moving)
    sends += moving
    coarse_shifts(dm, dm_recv)
    total = None
    for bb in range(3):
        for aa in range(3):
            left = clines(dm, bb - 1, hy, aa * width, (aa + 1) * width)
            term = dot_t(left, b_mid[3 * (2 - bb) + 2 - aa])
            total = term if total is None else total + term
    d_coarse = d_middle.reshape(hy + 2, hx, width)[1 : hy + 1].reshape(hy * hx, width)
    d_coarse = d_coarse + total
    slope = ds_pool.reshape(hy + 4, hx, width)[2 : hy + 2].reshape(hy * hx, width)
    d_pool = (d_coarse * slope).astype(BF16)
    backs = [[dot_t(d_pool, p_mat[2 * ii + jj]) for jj in range(2)] for ii in range(2)]
    d_hidden = frame(d_up, 0, ys) + woven(backs, ys)
    d_down = (d_hidden * frame(ds_down, 0, ys)).astype(BF16)
    dd[0, PAD : PAD + ys, :, width : 2 * width] = d_down

    sends += red0.across()
    row = conv_grad(
        [turned(lines(dd, 0, first, chunk, width, 2 * width)) for first in cuts],
        lambda cut, aa, bb: fine_tap(fc, 0, cut, aa, bb),
        planes, cf, width, Packer(sum2, 0, cf),
    )
    row = pair_grad(
        turned(d_pool),
        [groups(frame(hid, 0, ys), ys, ii, jj) for ii in range(2) for jj in range(2)],
        half, cc, width, Packer(sum2, row, cc),
    )
    padded_tail(sum2, row, 2)
    red2 = Reduction(2, sum2, got2, mid2, sizes[0] + sizes[1])
    sends += red2.scatter()
    fine_edges(dd, dd_send, False)
    moving = around(4, dd_send, dd_recv, 0)
    for spot, dy, first, target in ((6, -1, 0, ys), (7, 1, ys - 1, -1)):
        moving.append(
            send(
                dd.at[0, PAD + first : PAD + first + 1, :, width : 2 * width],
                dd.at[0, PAD + target : PAD + target + 1, :, width : 2 * width],
                ex_send.at[4, spot], ex_recv.at[4, spot], 0, dy,
            )
        )
    sends += red1.across()

    def finish(buf, index, rcv, value_of, target):
        fine_shifts(buf, 0, fine_halo(rcv))
        for first in cuts:
            own = lines(fc, index, first, chunk, width, 2 * width).astype(F32)
            hid[PAD + first : PAD + first + chunk] = (
                (own + value_of(first)).astype(BF16).astype(F32).reshape(chunk, xs, width)
            )
        value = frame(hid, 0, ys).reshape(ys * xs, width).astype(BF16)
        target[...] = dot(back[...], value).astype(BF16)

    arrive(skips)
    sends += skips
    finish(sk, 0, sk_recv, lambda first: conv(sk, 0, first, chunk, b_up), out_s)
    stores = []

    def store(src, dst):
        copy = pltpu.make_async_copy(src, dst, out_sem.at[len(stores)])
        copy.start()
        stores.append(copy)

    store(out_s, out_hbm)
    sends += red2.across()
    sends += red0.gather()
    sends += red1.gather()
    arrive(moving)
    sends += moving
    finish(dd, 1, dd_recv, lambda first: conv_t(dd, 0, first, chunk, b_down), gf_s)
    store(gf_s, gf_hbm)
    sends += red2.gather()
    for red in (red0, red1, red2):
        arrive(red.copies)
        rows = pl.ds(red.base, sizes[red.group])
        store(grads.at[rows, :], grads_hbm.at[rows, :])
    for copy in sends:
        copy.wait_send()
    for copy in stores:
        copy.wait()


def last_kernel(
    dims, out_in, gf_in, grads_in, output, grad_fields, g_down, g_pool, g_mid, g_unpool, g_up,
    st_out, st_gf, grads, st_down, st_pool, st_mid, st_unpool, st_up, in_sem, out_sem,
):
    nx, ny, xs, ys, cf, cc, planes, scale, sizes = dims
    loads = [
        pltpu.make_async_copy(src, dst, in_sem.at[spot])
        for spot, (src, dst) in enumerate(((grads_in, grads), (out_in, st_out), (gf_in, st_gf)))
    ]
    for load in loads:
        load.start()
    stores = []

    def store(src, dst):
        copy = pltpu.make_async_copy(src, dst, out_sem.at[len(stores)])
        copy.start()
        stores.append(copy)

    loads[0].wait()
    turned_blocks(grads, 0, cc, st_mid)
    store(st_mid, g_mid)
    loads[1].wait()
    store(st_out, output)
    loads[2].wait()
    store(st_gf, grad_fields)
    row = sizes[0]
    for block in range(st_up.shape[0] // cf):
        first = block * cf
        spot = block % (LANES // cf)
        if spot == 0:
            held = grads[row : row + cf, :].astype(F32)
            row += cf
        moved = held if spot == 0 else pltpu.roll(held, LANES - spot * cf, 1)
        st_up[first : first + cf, :] = moved[:, :cf]
    store(st_up, g_up)
    turned_blocks(grads, row, cc, st_unpool)
    store(st_unpool, g_unpool)
    row = turned_blocks(grads, sizes[0] + sizes[1], cf, st_down)
    store(st_down, g_down)
    turned_blocks(grads, row, cc, st_pool)
    store(st_pool, g_pool)
    for copy in stores:
        copy.wait()


def per_device(dims, fields, w_down, w_pool, w_mid, w_unpool, w_up, cotangent):
    nx, ny, xs, ys, cf, cc, planes, scale, sizes = dims
    hx, hy = xs // 2, ys // 2
    width = planes * cf
    hbm = pl.BlockSpec(memory_space=pl.ANY)
    tall, tall_c = ys + 2 * PAD, hy + 2 * CPAD

    def fine(lead=1):
        return pltpu.VMEM((lead, tall, xs, 3 * width), BF16)

    def coarse():
        return pltpu.VMEM((tall_c, hx, 3 * width), F32)

    def line(*shape):
        return pltpu.VMEM((2,) + shape + (width,), BF16)

    def sems(*shape):
        return pltpu.SemaphoreType.DMA(shape)

    def f32(*shape):
        return jax.ShapeDtypeStruct(shape, F32)

    def stage(values):
        return [pltpu.VMEM(value.shape, value.dtype) for value in values]

    rows = [size // nx for size in sizes]
    flat = jax.ShapeDtypeStruct((xs * ys, width), BF16)
    kept = ys + 2 * ROWS
    weights = (
        w_down.reshape(-1, cf),
        w_pool.reshape(-1, cc),
        w_mid.reshape(-1, cc),
        jnp.swapaxes(w_unpool, 3, 4).reshape(-1, cc),
        w_up.reshape(-1, cf),
    )
    total = jax.ShapeDtypeStruct((sum(sizes), LANES), BF16)
    mains = pl.pallas_call(
        functools.partial(main_kernel, dims),
        out_shape=(flat, flat, total),
        in_specs=[hbm] * 7,
        out_specs=(hbm,) * 3,
        scratch_shapes=[
            *stage((flat, flat, total)),
            pltpu.VMEM((2, xs * ys, width), BF16),
            *stage(weights),
            fine(2), fine(), fine(), coarse(), coarse(),
            line(kept), line(kept), line(2 * ROWS), line(2 * ROWS),
            line(2, kept), line(kept), line(kept), line(2 * ROWS), line(2 * ROWS),
            pltpu.VMEM((9, width, width), BF16),
            pltpu.VMEM((9, width, width), BF16),
            pltpu.VMEM((9, width, width), BF16),
            pltpu.VMEM((4, width, width), BF16),
            pltpu.VMEM((4, width, width), BF16),
            pltpu.VMEM((2 * ROWS * xs, ROWS * xs), BF16),
            pltpu.VMEM((2, ROWS * xs, 2 * ROWS), BF16),
            pltpu.VMEM((2 * tall_c * hx, tall_c * hx), BF16),
            pltpu.VMEM((2, tall_c * hx, 2 * ROWS), BF16),
            pltpu.VMEM((xs * ys, xs * ys), BF16),
            pltpu.VMEM((xs * ys, xs * ys), BF16),
            *[pltpu.VMEM((tall, xs, width), F32) for _ in range(4)],
            *[pltpu.VMEM((size, LANES), BF16) for size in sizes],
            *[pltpu.VMEM((nx - 1, row, LANES), BF16) for row in rows],
            *[pltpu.VMEM((ny, row, LANES), BF16) for row in rows],
            sems(7), sems(5),
            sems(5, 10), sems(5, 10),
            sems(3, nx - 1), sems(3, nx - 1),
            sems(3, ny - 1), sems(3, ny - 1),
            sems(3, nx - 1), sems(3, nx - 1),
        ],
        compiler_params=pltpu.CompilerParams(
            collective_id=0, has_side_effects=True, vmem_limit_bytes=60 << 20
        ),
        name="unet",
    )(fields.reshape(xs * ys, width), *weights, cotangent.reshape(xs * ys, width))

    results = (
        flat, flat, f32(27 * cf, cf), f32(8 * cf, cc), f32(27 * cc, cc), f32(8 * cf, cc),
        f32(27 * cf, cf),
    )
    output, grad_fields, g_down, g_pool, g_mid, g_unpool, g_up = pl.pallas_call(
        functools.partial(last_kernel, dims),
        out_shape=results,
        in_specs=[hbm] * 3,
        out_specs=(hbm,) * 7,
        scratch_shapes=[*stage((flat, flat, total)), *stage(results[2:]), sems(3), sems(7)],
        name="layouts",
    )(*mains)
    swapped = w_unpool.shape[:3] + (cf, cc)
    return (
        output.reshape(fields.shape),
        grad_fields.reshape(fields.shape),
        g_down.reshape(w_down.shape),
        g_pool.reshape(w_pool.shape),
        g_mid.reshape(w_mid.shape),
        jnp.swapaxes(g_unpool.reshape(swapped), 3, 4),
        g_up.reshape(w_up.shape),
    )


def solution(mesh):
    nx, ny = mesh.shape["gx"], mesh.shape["gy"]

    def whole(fields, w_down, w_pool, w_mid, w_unpool, w_up, cotangent):
        cf, cc = w_down.shape[3], w_mid.shape[3]
        xs, ys = fields.shape[0] // nx, fields.shape[1] // ny
        planes = fields.shape[2] // cf
        scale = 1.0 / math.sqrt(fields.shape[0] * fields.shape[1] * planes)

        def blocks(taps, chan):
            return -(-taps * chan // LANES) * chan

        fine_rows = blocks(27, cf)
        pair_rows = 4 * cc * 2 * cf // LANES
        unit = ROWS * nx
        sizes = tuple(
            -(-rows // unit) * unit
            for rows in (blocks(27, cc), fine_rows + pair_rows, fine_rows + pair_rows)
        )
        dims = (nx, ny, xs, ys, cf, cc, planes, scale, sizes)
        placed = (P("gx", "gy", None), P(), P(), P(), P(), P(), P("gx", "gy", None))
        return jax.shard_map(
            functools.partial(per_device, dims),
            mesh=mesh,
            in_specs=placed,
            out_specs=(P("gx", "gy", None), P("gx", "gy", None), P(), P(), P(), P(), P()),
            check_vma=False,
        )(fields, w_down, w_pool, w_mid, w_unpool, w_up, cotangent)

    return whole
```
